256 devices in a mesh: gx: 32 (over y_lo, z, core), gy: 8 (over y_hi, x).
Axes of the slice: x: 4, y: 4 (y_hi: 2, y_lo: 2; y = y_hi * 2 + y_lo), z: 8, core: 2. Of those that a mesh axis runs over, the one named last changes fastest.
Arguments:
- input_one: float32 [32, 2, 128, 1024], P(None, None, 'gx', 'gy'), may hold values from -6 to 6
- input_two: float32 [32, 2, 128, 1024], P(None, None, 'gx', 'gy'), may hold values from -6 to 6
- input_three: float32 [32, 2, 128, 1024], P(None, None, 'gx', 'gy'), may hold values from -6 to 6
- cotangent: float32 [32, 2, 128, 1024], P(None, None, 'gx', 'gy'), may hold values from -6 to 6
- kernel_one: float32 [27, 32, 32], replicated, may hold values from -0.21875 to 0.21875
- kernel_two: float32 [27, 32, 32], replicated, may hold values from -0.21875 to 0.21875
- kernel_three: float32 [27, 32, 32], replicated, may hold values from -0.21875 to 0.21875
Outputs:
- grad_input: float32 [32, 2, 128, 1024], P(None, None, 'gx', 'gy')
- grad_kernel_one: float32 [27, 32, 32], replicated
- grad_kernel_two: float32 [27, 32, 32], replicated
- grad_kernel_three: float32 [27, 32, 32], replicated
The draws below stay inside these ranges and needn't reach their ends.
All inputs are finite; a program needn't handle non-finite values.
Results may differ from the reference program's by a relative error of at most 0.00013.
Values sent between devices are 32-bit elements; how exact they have to be, the bound alone decides.
A program may use at most 64 MiB of HBM per device.

```python
import math
import jax
import jax.numpy as jnp
from jax import lax

C = 32
NZ = 2
NX = 128
NY = 1024


def shard_levels(own_key, extent, split, low, top_value):
    factor_of, own = 1.0, jax.random.fold_in(own_key, 6)
    for axis_at, blocks in split:
        heights = jnp.exp(jax.random.uniform(jax.random.fold_in(own, axis_at), (blocks,), jnp.float32, low / len(split), top_value / len(split)))
        factor_of = factor_of * jnp.repeat(heights, extent[axis_at] // blocks).reshape([-1 if axis == axis_at else 1 for axis in range(len(extent))])
    return factor_of


def normal_values(key, shape, spread, reach, shards=(), kind=jnp.bfloat16):
    entries = spread * jax.random.normal(key, shape, jnp.float32)
    if shards:
        entries = entries * shard_levels(key, shape, shards, -0.22, 0.18)
    return jnp.clip(entries, -reach, reach).astype(kind)


def setup_inputs(seed: int = 0) -> dict:
    key_list = jax.random.split(jax.random.key(seed), 8)
    return {
        "input_one": normal_values(key_list[0], (C, NZ, NX, NY), 1.0, 6.0, ((2, 32), (3, 8)), jnp.float32),
        "input_two": normal_values(key_list[1], (C, NZ, NX, NY), 1.0, 6.0, ((2, 32), (3, 8)), jnp.float32),
        "input_three": normal_values(key_list[2], (C, NZ, NX, NY), 1.0, 6.0, ((2, 32), (3, 8)), jnp.float32),
        "cotangent": normal_values(key_list[3], (C, NZ, NX, NY), 1.0, 6.0, ((2, 32), (3, 8)), jnp.float32),
        "kernel_one": normal_values(key_list[4], (27, C, C), (27 * C) ** -0.5, 0.21875, (), jnp.float32),
        "kernel_two": normal_values(key_list[5], (27, C, C), (27 * C) ** -0.5, 0.21875, (), jnp.float32),
        "kernel_three": normal_values(key_list[6], (27, C, C), (27 * C) ** -0.5, 0.21875, (), jnp.float32),
    }


inv_root_two = 0.7071067811865476
inv_root_two_pi = 0.3989422804014327

def gelu_slope(value):
    normal_cdf = 0.5 * (1.0 + jax.scipy.special.erf(value * inv_root_two))
    density = jnp.exp(-0.5 * value * value) * inv_root_two_pi
    return normal_cdf + value * density

def conv_taps(padded, kernel, depth, rows, cols):
    total = None
    for tap in range(27):
        a, b, c = (tap // 9, tap // 3 % 3, tap % 3)
        window = padded[:, a:a + depth, b:b + rows, c:c + cols]
        term = jnp.einsum('oi,izxy->ozxy', kernel[tap], window, precision=lax.Precision.HIGHEST)
        total = term if total is None else total + term
    return total

def back_taps(padded, kernel, depth, rows, cols):
    total = None
    for tap in range(27):
        a, b, c = (tap // 9, tap // 3 % 3, tap % 3)
        window = padded[:, 2 - a:2 - a + depth, 2 - b:2 - b + rows, 2 - c:2 - c + cols]
        term = jnp.einsum('oi,ozxy->izxy', kernel[tap], window, precision=lax.Precision.HIGHEST)
        total = term if total is None else total + term
    return total

def kernel_terms(padded, slope_grad, depth, rows, cols):
    parts = []
    for tap in range(27):
        a, b, c = (tap // 9, tap // 3 % 3, tap % 3)
        window = padded[:, a:a + depth, b:b + rows, c:c + cols]
        parts.append(jnp.einsum('ozxy,izxy->oi', slope_grad, window, precision=lax.Precision.HIGHEST))
    return jnp.stack(parts, axis=0)

def reference(input_one, input_two, input_three, cotangent, kernel_one, kernel_two, kernel_three):
    depth, rows, cols = (input_one.shape[1], input_one.shape[2], input_one.shape[3])
    factor = 1.0 / math.sqrt(depth * rows * cols)
    widths = ((0, 0), (1, 1), (1, 1), (1, 1))
    grad = cotangent
    results = []
    for field, kernel in ((input_three, kernel_three), (input_two, kernel_two), (input_one, kernel_one)):
        padded = jnp.pad(field, widths)
        pre = conv_taps(padded, kernel, depth, rows, cols)
        slope_grad = grad * gelu_slope(pre)
        results.append(kernel_terms(padded, slope_grad, depth, rows, cols) * factor)
        grad = back_taps(jnp.pad(slope_grad, widths), kernel, depth, rows, cols)
    return (grad, results[2], results[1], results[0])
```

```python
import functools
import math

import jax
import jax.numpy as jnp
from jax import lax
from jax.experimental import pallas as pl
from jax.experimental.pallas import tpu as pltpu
from jax.sharding import PartitionSpec as P

MESH = pl.DeviceIdType.MESH
F32, BF16 = jnp.float32, jnp.bfloat16
INV_ROOT_TWO = 0.7071067811865476
INV_ROOT_TWO_PI = 0.3989422804014327
SIDES = ((-1, -1), (0, -1), (1, -1), (-1, 1), (0, 1), (1, 1))


def gelu_slope(value):
    normal_cdf = 0.5 * (1.0 + lax.erf(value * INV_ROOT_TWO))
    density = jnp.exp(-0.5 * value * value) * INV_ROOT_TWO_PI
    return normal_cdf + value * density


def split(value):
    high = value.astype(BF16)
    low = (value - high.astype(F32)).astype(BF16)
    return high, low


def roll(value, shift):
    shift = shift % 128
    return value if shift == 0 else pltpu.roll(value, shift, 1)


def lanes(rows):
    return lax.broadcasted_iota(jnp.int32, (rows, 128), 1)


def step_kernel(
    dims, x3_in, cot_in, x2_in, x1_in, k3_in, k2_in, k1_in,
    gin_ref, red_ref,
    x3, cot, x2, x1, k3, k2, k1,
    send, recv, field, weights, hmat, prod, slope,
    part, rs_recv, z_recv, ag_recv,
    load_sem, halo_send, halo_recv, rs_send_sem, rs_recv_sem, z_send_sem, z_recv_sem, ag_send_sem, ag_recv_sem,
):
    gxn, gyn, zn, ylo = dims
    members = ylo * 2 * gyn
    per = 32 // members
    gx, gy = lax.axis_index("gx"), lax.axis_index("gy")
    core, my_z, my_y = gx % 2, gx // 2 % zn, gx // (2 * zn)
    me = (my_y * 2 + core) * gyn + gy

    def member(m):
        row = m // gyn
        return (row // 2 * (2 * zn) + my_z * 2 + row % 2, m % gyn)

    def z_peer(k):
        return (my_y * (2 * zn) + k * 2 + core, gy)

    def near(n, side):
        return ((gx + n + gxn) % gxn, (gy + side + gyn) % gyn)

    loads = []
    for i, (src, dst) in enumerate(
        ((x3_in, x3), (k3_in, k3), (cot_in, cot), (x2_in, x2), (x1_in, x1), (k2_in, k2), (k1_in, k1))
    ):
        copy = pltpu.make_async_copy(src, dst, load_sem.at[i])
        copy.start()
        loads.append(copy)

    barrier = pltpu.get_barrier_semaphore()
    around = [near(n, s) for n, s in SIDES] + [near(-1, 0), near(1, 0)]
    for device in around:
        pl.semaphore_signal(barrier, inc=1, device_id=device, device_id_type=MESH)

    def greet_member(k, carry):
        pl.semaphore_signal(barrier, inc=1, device_id=member((me + k) % members), device_id_type=MESH)
        return carry

    def greet_z(k, carry):
        pl.semaphore_signal(barrier, inc=1, device_id=z_peer((my_z + k) % zn), device_id_type=MESH)
        return carry

    lax.fori_loop(1, members, greet_member, 0)
    lax.fori_loop(1, zn, greet_z, 0)

    up = (gx > 0).astype(F32)
    down = (gx < gxn - 1).astype(F32)
    left = (gy > 0).astype(F32)
    right = (gy < gyn - 1).astype(F32)
    lane8, lane32 = lanes(8), lanes(32)
    zero32 = jnp.zeros((32, 128), F32)

    for bi in range(4):
        for part_row in (0, 256):
            for z in range(2):
                base = part_row + z * 128 + 96
                field[bi, base : base + 32, :] = jnp.zeros((32, 640), BF16)

    def load_tiles(ref):
        return [[ref[pl.ds(z * 4 + x, 32, stride=8), :] for x in range(4)] for z in range(2)]

    def edge_columns(tiles):
        packed = []
        for z in range(2):
            total = zero32
            for x in range(4):
                keep = (lane32 == 8 * x) | (lane32 == (8 * x - 1) % 128)
                total = jnp.where(keep, roll(tiles[z][x], 8 * x), total)
            packed.append(total)
        return packed

    def fill_send(f, tiles, packed):
        for z in range(2):
            send[f, z * 32 : z * 32 + 32, :] = tiles[z][0]
            send[f, 64 + z * 32 : 96 + z * 32, :] = tiles[z][3]
        squeezed = None
        for z in range(2):
            for v in range(4):
                term = roll(packed[z][8 * v : 8 * v + 8], 2 * v + 64 * z)
                squeezed = term if squeezed is None else squeezed + term
        send[f, 128:136, :] = squeezed

    def fill_own(bi, tiles):
        for z in range(2):
            for x_in in range(4):
                high, low = split(tiles[z][x_in])
                for b in range(3):
                    x = x_in + 1 - b
                    if 0 <= x < 4:
                        row, col = z * 128 + b * 32, x * 128
                        field[bi, row : row + 32, col : col + 128] = high
                        field[bi, 256 + row : 288 + row, col : col + 128] = low

    def halo_copies(f):
        copies = []

        def add(lo, hi, at, device):
            copies.append(
                pltpu.make_async_remote_copy(
                    src_ref=send.at[f, pl.ds(lo, hi - lo)],
                    dst_ref=recv.at[f, pl.ds(at, hi - lo)],
                    send_sem=halo_send.at[f],
                    recv_sem=halo_recv.at[f],
                    device_id=device,
                    device_id_type=MESH,
                )
            )

        for k, (n, s) in enumerate(SIDES):
            add(128, 136, 128 + 8 * k, near(-n, -s))
        add(64, 128, 0, near(1, 0))
        add(0, 64, 64, near(-1, 0))
        return copies

    def start_halo(f):
        for copy in halo_copies(f):
            copy.start()

    def whole_halo(f):
        return pltpu.make_async_remote_copy(
            src_ref=recv.at[f], dst_ref=recv.at[f], send_sem=halo_send.at[f], recv_sem=halo_recv.at[f],
            device_id=near(1, 0), device_id_type=MESH,
        )

    def fill_halo(bi, f):
        for z in range(2):
            for at, b, x, ok in ((0, 0, 0, up), (64, 2, 3, down)):
                high, low = split(recv[f, at + z * 32 : at + z * 32 + 32, :] * ok)
                row, col = z * 128 + b * 32, x * 128
                field[bi, row : row + 32, col : col + 128] = high
                field[bi, 256 + row : 288 + row, col : col + 128] = low
        first = ((lane8 & 63) >= 55) & ((lane8 & 63) <= 62)
        last = ((lane8 & 63) >= 31) & ((lane8 & 63) <= 38)
        merged = []
        for k, ok in ((0, left), (3, right)):
            tile = [recv[f, 128 + 8 * (k + j) : 136 + 8 * (k + j), :] for j in range(3)]
            total = tile[1]
            total = total + jnp.where(first, roll(tile[0], 96), 0.0) * up
            total = total + jnp.where(last, roll(tile[2], 32), 0.0) * down
            merged.append(total * ok)
        both = jnp.where(lane8 % 2 == 1, roll(merged[0], 2), merged[1])
        for z in range(2):
            for b in range(3):
                tile = jnp.concatenate([roll(both, 7 - 2 * v - 64 * z - 8 * b) for v in range(4)], axis=0)
                high, low = split(tile)
                row = z * 128 + b * 32
                field[bi, row : row + 32, 512:640] = high
                field[bi, 256 + row : 288 + row, 512:640] = low

    def row_block(kernel, a, c):
        return jnp.concatenate(
            [kernel[9 * a + 3 * b + c] for b in range(3)] + [jnp.zeros((32, 32), F32)], axis=1
        )

    def store_weights(wi, row, col, tile):
        high, low = split(tile)
        weights[wi, row : row + 32, col : col + 128] = high
        weights[wi, row : row + 32, 256 + col : 384 + col] = high
        weights[wi, row : row + 32, 512 + col : 640 + col] = low

    def build_weights(layer, kernel):
        for a in range(3):
            blocks = [row_block(kernel, a, c) for c in range(3)]
            flipped = jnp.concatenate(blocks + [zero32], axis=0).T
            for c in range(3):
                back = jnp.concatenate(
                    [
                        flipped[(2 - b) * 32 : (3 - b) * 32, (2 - c) * 32 : (3 - c) * 32]
                        for b in range(3)
                    ]
                    + [jnp.zeros((32, 32), F32)],
                    axis=1,
                )
                for z in range(2):
                    zp = a + z - 1
                    if 0 <= zp < 2:
                        store_weights(layer, c * 64 + z * 32, zp * 128, blocks[c])
                        store_weights(3 + layer, c * 64 + zp * 32, z * 128, back)

    def conv(wi, bi):
        for lo, hi in ((0, 256), (256, 512), (512, 640)):
            prod[:, lo:hi] = jnp.dot(
                weights[wi, :, 0:512], field[bi, :, lo:hi], preferred_element_type=F32
            ) + jnp.dot(weights[wi, :, 512:768], field[bi, 0:256, lo:hi], preferred_element_type=F32)
        out = []
        for z in range(2):
            row = z * 32
            edge = jnp.where(
                lane32 % 8 == 0, prod[row : row + 32, 512:640], prod[128 + row : 160 + row, 512:640]
            )
            tiles = []
            for x in range(4):
                col = x * 128
                at_edge = roll(edge, -8 * x)
                before = roll(prod[row : row + 32, col : col + 128], 1)
                after = roll(prod[128 + row : 160 + row, col : col + 128], -1)
                tiles.append(
                    prod[64 + row : 96 + row, col : col + 128]
                    + jnp.where(lane32 == 0, at_edge, before)
                    + jnp.where(lane32 == 127, at_edge, after)
                )
            out.append(tiles)
        return out

    def store_h(c, z, col, tile):
        high, low = split(tile)
        row = c * 64 + z * 32
        hmat[row : row + 32, col : col + 128] = high
        hmat[192 + row : 224 + row, col : col + 128] = low

    def kernel_grad(layer, bi, tiles, packed):
        for z in range(2):
            for x in range(4):
                col = x * 128
                store_h(0, z, col, jnp.where(lane32 == 127, 0.0, roll(tiles[z][x], -1)))
                store_h(1, z, col, tiles[z][x])
                store_h(2, z, col, jnp.where(lane32 == 0, 0.0, roll(tiles[z][x], 1)))
            store_h(0, z, 512, jnp.where(lane32 % 8 == 0, packed[z], 0.0))
            store_h(1, z, 512, zero32)
            store_h(2, z, 512, jnp.where(lane32 % 8 == 7, packed[z], 0.0))
        contract = (((1,), (1,)), ((), ()))
        main = lax.dot_general(hmat[...], field[bi, 0:256, :], contract, preferred_element_type=F32)
        rest = lax.dot_general(hmat[0:192, :], field[bi, 256:512, :], contract, preferred_element_type=F32)
        total = main[0:192] + main[192:384] + rest
        blocks = []
        for c in range(3):
            top, low = total[c * 64 : c * 64 + 32], total[c * 64 + 32 : c * 64 + 64]
            blocks += [low[:, 0:128], top[:, 0:128] + low[:, 128:256], top[:, 128:256]]
        for j in range(8):
            block = blocks[j]
            if j < 3:
                block = jnp.where(lane32 >= 96, roll(blocks[8], 96 - 32 * j), block)
            part[layer, 4 * j : 4 * j + 4] = block.reshape(4, 8, 128)

    def group_copy(src, dst, send_sem, recv_sem, device):
        return pltpu.make_async_remote_copy(
            src_ref=src, dst_ref=dst, send_sem=send_sem, recv_sem=recv_sem, device_id=device, device_id_type=MESH
        )

    def rs_start(layer):
        def body(k, carry):
            m = (me + k) % members
            group_copy(
                part.at[layer, pl.ds(m * per, per)], rs_recv.at[layer, pl.ds(me * per, per)],
                rs_send_sem.at[layer], rs_recv_sem.at[layer], member(m),
            ).start()
            return carry

        lax.fori_loop(1, members, body, 0)
        rs_recv[layer, pl.ds(me * per, per)] = part[layer, pl.ds(me * per, per)]

    def rs_wait(layer):
        count = (members - 1) * per
        return group_copy(
            part.at[layer, pl.ds(0, count)], rs_recv.at[layer, pl.ds(0, count)],
            rs_send_sem.at[layer], rs_recv_sem.at[layer], near(1, 0),
        )

    def z_start(layer):
        rs_wait(layer).wait_recv()
        total = rs_recv[layer, 0:per]
        for m in range(1, members):
            total = total + rs_recv[layer, m * per : m * per + per]
        z_recv[layer, my_z] = total

        def body(k, carry):
            group_copy(
                z_recv.at[layer, my_z], z_recv.at[layer, my_z],
                z_send_sem.at[layer], z_recv_sem.at[layer], z_peer((my_z + k) % zn),
            ).start()
            return carry

        lax.fori_loop(1, zn, body, 0)

    def z_wait(layer):
        return group_copy(
            z_recv.at[layer, pl.ds(0, zn - 1)], z_recv.at[layer, pl.ds(0, zn - 1)],
            z_send_sem.at[layer], z_recv_sem.at[layer], near(1, 0),
        )

    def ag_start(layer):
        z_wait(layer).wait_recv()
        total = z_recv[layer, 0]
        for k in range(1, zn):
            total = total + z_recv[layer, k]
        mine = pl.ds(me * per, per)
        ag_recv[layer, mine] = total

        def body(k, carry):
            group_copy(
                ag_recv.at[layer, mine], ag_recv.at[layer, mine],
                ag_send_sem.at[layer], ag_recv_sem.at[layer], member((me + k) % members),
            ).start()
            return carry

        lax.fori_loop(1, members, body, 0)

    def ag_wait(layer):
        count = pl.ds(0, (members - 1) * per)
        return group_copy(
            ag_recv.at[layer, count], ag_recv.at[layer, count],
            ag_send_sem.at[layer], ag_recv_sem.at[layer], near(1, 0),
        )

    def finish(layer):
        ag_wait(layer).wait_recv()
        red_ref[layer] = ag_recv[layer]

    loads[0].wait()
    tiles = load_tiles(x3)
    fill_send(0, tiles, edge_columns(tiles))
    pl.semaphore_wait(barrier, len(around) + members - 1 + zn - 1)
    start_halo(0)
    fill_own(0, tiles)
    for f, ref, at in ((1, x2, 3), (2, x1, 4)):
        loads[at].wait()
        tiles = load_tiles(ref)
        fill_send(f, tiles, edge_columns(tiles))
        start_halo(f)
        fill_own(f, tiles)
    loads[1].wait()
    build_weights(0, k3)
    loads[2].wait()
    loads[5].wait()
    loads[6].wait()
    grad = load_tiles(cot)

    for layer in range(3):
        if layer == 0:
            whole_halo(0).wait_recv()
            fill_halo(0, 0)
            pre = conv(0, 0)
            mult = [[gelu_slope(pre[z][x]) for x in range(4)] for z in range(2)]
        else:
            mult = [
                [slope[layer - 1, (z * 4 + x) * 32 : (z * 4 + x) * 32 + 32, :] for x in range(4)] for z in range(2)
            ]
        h = [[grad[z][x] * mult[z][x] for x in range(4)] for z in range(2)]
        packed = edge_columns(h)
        fill_send(3 + layer, h, packed)
        start_halo(3 + layer)
        fill_own(3, h)
        kernel_grad(layer, layer, h, packed)
        rs_start(layer)
        if layer < 2:
            build_weights(layer + 1, (k2, k1)[layer])
            whole_halo(layer + 1).wait_recv()
            fill_halo(layer + 1, layer + 1)
            pre = conv(layer + 1, layer + 1)
            for z in range(2):
                for x in range(4):
                    at = (z * 4 + x) * 32
                    slope[layer, at : at + 32, :] = gelu_slope(pre[z][x])
        whole_halo(3 + layer).wait_recv()
        fill_halo(3, 3 + layer)
        grad = conv(3 + layer, 3)
        if layer == 1:
            z_start(0)
    for z in range(2):
        for x in range(4):
            gin_ref[pl.ds(z * 4 + x, 32, stride=8), :] = grad[z][x]
    z_start(1)
    ag_start(0)
    z_start(2)
    ag_start(1)
    finish(0)
    ag_start(2)
    finish(1)
    finish(2)
    for f in range(6):
        whole_halo(f).wait_send()
    for layer in range(3):
        rs_wait(layer).wait_send()
        z_wait(layer).wait_send()
        ag_wait(layer).wait_send()


def unpack_kernel(factor, gin_in, red_ref, gin_ref, out3, out2, out1):
    gin_ref[...] = gin_in[...]
    for layer, out in enumerate((out3, out2, out1)):
        for a in range(3):
            for b in range(3):
                for c in range(3):
                    j = c * 3 + a
                    row, col = (j * 32, b * 32) if j < 8 else (b * 32, 96)
                    out[9 * a + 3 * b + c] = red_ref[layer, row : row + 32, col : col + 32] * factor


def per_device(dims, factor, x1, x2, x3, cot, k1, k2, k3):
    flat = [v.reshape(256, 128) for v in (x3, cot, x2, x1)]
    vmem = pl.BlockSpec(memory_space=pltpu.VMEM)
    anywhere = pl.BlockSpec(memory_space=pl.ANY)
    members = dims[3] * 2 * dims[1]
    per = 32 // members
    dma = pltpu.SemaphoreType.DMA
    gin, red = pl.pallas_call(
        functools.partial(step_kernel, dims),
        out_shape=(jax.ShapeDtypeStruct((256, 128), F32), jax.ShapeDtypeStruct((3, 32, 8, 128), F32)),
        in_specs=[anywhere] * 7,
        out_specs=(vmem, vmem),
        scratch_shapes=[pltpu.VMEM((256, 128), F32)] * 4
        + [pltpu.VMEM((27, 32, 32), F32)] * 3
        + [
            pltpu.VMEM((6, 136, 128), F32),
            pltpu.VMEM((6, 176, 128), F32),
            pltpu.VMEM((4, 512, 640), BF16),
            pltpu.VMEM((6, 192, 768), BF16),
            pltpu.VMEM((384, 640), BF16),
            pltpu.VMEM((192, 640), F32),
            pltpu.VMEM((2, 256, 128), F32),
            pltpu.VMEM((3, 32, 8, 128), F32),
            pltpu.VMEM((3, 32, 8, 128), F32),
            pltpu.VMEM((3, dims[2], per, 8, 128), F32),
            pltpu.VMEM((3, 32, 8, 128), F32),
            dma((7,)), dma((6,)), dma((6,)), dma((3,)), dma((3,)), dma((3,)), dma((3,)), dma((3,)), dma((3,)),
        ],
        compiler_params=pltpu.CompilerParams(
            collective_id=0, has_side_effects=True, vmem_limit_bytes=67043328
        ),
        name="step",
    )(*flat, k3, k2, k1)
    shape = jax.ShapeDtypeStruct(k1.shape, F32)
    gin, out3, out2, out1 = pl.pallas_call(
        functools.partial(unpack_kernel, factor),
        out_shape=(jax.ShapeDtypeStruct((256, 128), F32), shape, shape, shape),
        in_specs=[vmem] * 2,
        out_specs=(vmem,) * 4,
        name="unpack",
    )(gin, red.reshape(3, 256, 128))
    return gin.reshape(x1.shape), out1, out2, out3


def solution(mesh):
    gxn, gyn = mesh.shape["gx"], mesh.shape["gy"]
    zn = min(8, gxn // 2)
    dims = (gxn, gyn, zn, gxn // (2 * zn))
    factor = 1.0 / math.sqrt(2 * 4 * 128 * gxn * gyn)
    placed = P(None, None, "gx", "gy")
    return jax.shard_map(
        functools.partial(per_device, dims, factor),
        mesh=mesh,
        in_specs=(placed,) * 4 + (P(),) * 3,
        out_specs=(placed, P(), P(), P()),
        check_vma=False,
    )
```

```python
import functools
import math

import jax
import jax.numpy as jnp
from jax import lax
from jax.experimental import pallas as pl
from jax.experimental.pallas import tpu as pltpu
from jax.sharding import PartitionSpec as P

MESH = pl.DeviceIdType.MESH
F32, BF16 = jnp.float32, jnp.bfloat16
INV_ROOT_TWO = 0.7071067811865476
INV_ROOT_TWO_PI = 0.3989422804014327
SIDES = ((-1, -1), (0, -1), (1, -1), (-1, 1), (0, 1), (1, 1))


def gelu_slope(value):
    normal_cdf = 0.5 * (1.0 + lax.erf(value * INV_ROOT_TWO))
    density = jnp.exp(-0.5 * value * value) * INV_ROOT_TWO_PI
    return normal_cdf + value * density


def split(value):
    high = value.astype(BF16)
    low = (value - high.astype(F32)).astype(BF16)
    return high, low


def roll(value, shift):
    shift = shift % 128
    return value if shift == 0 else pltpu.roll(value, shift, 1)


def lanes(rows):
    return lax.broadcasted_iota(jnp.int32, (rows, 128), 1)


def step_kernel(
    dims, x3_in, cot_in, x2_in, x1_in, k3_in, k2_in, k1_in,
    gin_ref, red_ref,
    x3, cot, x2, x1, k3, k2, k1,
    send, recv, field, weights, hmat, prod, slope,
    part, rs_recv, z_recv, ag_recv,
    load_sem, halo_send, halo_recv, rs_send_sem, rs_recv_sem, z_send_sem, z_recv_sem, ag_send_sem, ag_recv_sem,
):
    gxn, gyn, zn, ylo = dims
    members = ylo * 2 * gyn
    per = 32 // members
    gx, gy = lax.axis_index("gx"), lax.axis_index("gy")
    core, my_z, my_y = lax.rem(gx, 2), lax.rem(lax.div(gx, 2), zn), lax.div(gx, 2 * zn)
    me = (my_y * 2 + core) * gyn + gy

    lines = []
    for ky in range(ylo):
        for kc in range(2):
            other_y, other_core = lax.rem(my_y + ky, ylo), lax.rem(core + kc, 2)
            lines.append((other_y * (2 * zn) + my_z * 2 + other_core, (other_y * 2 + other_core) * gyn))
    spots = [lax.rem(gy + k, gyn) for k in range(gyn)]
    peers = [((at, spot), base + spot) for spot in spots for at, base in lines][1:]
    z_peers = [(my_y * (2 * zn) + lax.rem(my_z + k, zn) * 2 + core, gy) for k in range(1, zn)]

    def near(n, side):
        return (lax.rem(gx + n + gxn, gxn), lax.rem(gy + side + gyn, gyn))

    loads = []
    for i, (src, dst) in enumerate(
        ((x3_in, x3), (k3_in, k3), (cot_in, cot), (x2_in, x2), (x1_in, x1), (k2_in, k2), (k1_in, k1))
    ):
        copy = pltpu.make_async_copy(src, dst, load_sem.at[i])
        copy.start()
        loads.append(copy)

    barrier = pltpu.get_barrier_semaphore()
    around = [near(n, s) for n, s in SIDES] + [near(-1, 0), near(1, 0)]
    greeted = around + [device for device, _ in peers] + z_peers
    for device in greeted:
        pl.semaphore_signal(barrier, inc=1, device_id=device, device_id_type=MESH)

    up = (gx > 0).astype(F32)
    down = (gx < gxn - 1).astype(F32)
    left = (gy > 0).astype(F32)
    right = (gy < gyn - 1).astype(F32)
    lane8, lane32 = lanes(8), lanes(32)
    zero32 = jnp.zeros((32, 128), F32)

    for bi in range(4):
        for part_row in (0, 256):
            for z in range(2):
                base = part_row + z * 128 + 96
                field[bi, base : base + 32, :] = jnp.zeros((32, 640), BF16)

    def load_tiles(ref):
        return [[ref[pl.ds(z * 4 + x, 32, stride=8), :] for x in range(4)] for z in range(2)]

    def edge_columns(tiles):
        packed = []
        for z in range(2):
            total = zero32
            for x in range(4):
                keep = (lane32 == 8 * x) | (lane32 == (8 * x - 1) % 128)
                total = jnp.where(keep, roll(tiles[z][x], 8 * x), total)
            packed.append(total)
        return packed

    def fill_send(f, tiles, packed):
        for z in range(2):
            send[f, z * 32 : z * 32 + 32, :] = tiles[z][0]
            send[f, 64 + z * 32 : 96 + z * 32, :] = tiles[z][3]
        squeezed = None
        for z in range(2):
            for v in range(4):
                term = roll(packed[z][8 * v : 8 * v + 8], 2 * v + 64 * z)
                squeezed = term if squeezed is None else squeezed + term
        send[f, 128:136, :] = squeezed

    def fill_own(bi, tiles):
        for z in range(2):
            for x_in in range(4):
                high, low = split(tiles[z][x_in])
                for b in range(3):
                    x = x_in + 1 - b
                    if 0 <= x < 4:
                        row, col = z * 128 + b * 32, x * 128
                        field[bi, row : row + 32, col : col + 128] = high
                        field[bi, 256 + row : 288 + row, col : col + 128] = low

    def halo_copies(f):
        copies = []

        def add(lo, hi, at, device):
            copies.append(
                pltpu.make_async_remote_copy(
                    src_ref=send.at[f, pl.ds(lo, hi - lo)],
                    dst_ref=recv.at[f, pl.ds(at, hi - lo)],
                    send_sem=halo_send.at[f],
                    recv_sem=halo_recv.at[f],
                    device_id=device,
                    device_id_type=MESH,
                )
            )

        for k, (n, s) in enumerate(SIDES):
            add(128, 136, 128 + 8 * k, near(-n, -s))
        add(64, 128, 0, near(1, 0))
        add(0, 64, 64, near(-1, 0))
        return copies

    def start_halo(f):
        for copy in halo_copies(f):
            copy.start()

    def whole_halo(f):
        return pltpu.make_async_remote_copy(
            src_ref=recv.at[f], dst_ref=recv.at[f], send_sem=halo_send.at[f], recv_sem=halo_recv.at[f],
            device_id=near(1, 0), device_id_type=MESH,
        )

    def halo_wait(f):
        whole_halo(f).wait_recv()

    def fill_halo(bi, f):
        for z in range(2):
            for at, b, x, ok in ((0, 0, 0, up), (64, 2, 3, down)):
                high, low = split(recv[f, at + z * 32 : at + z * 32 + 32, :] * ok)
                row, col = z * 128 + b * 32, x * 128
                field[bi, row : row + 32, col : col + 128] = high
                field[bi, 256 + row : 288 + row, col : col + 128] = low
        first = ((lane8 & 63) >= 55) & ((lane8 & 63) <= 62)
        last = ((lane8 & 63) >= 31) & ((lane8 & 63) <= 38)
        merged = []
        for k, ok in ((0, left), (3, right)):
            tile = [recv[f, 128 + 8 * (k + j) : 136 + 8 * (k + j), :] for j in range(3)]
            total = tile[1]
            total = total + jnp.where(first, roll(tile[0], 96), 0.0) * up
            total = total + jnp.where(last, roll(tile[2], 32), 0.0) * down
            merged.append(total * ok)
        both = jnp.where(lane8 % 2 == 1, roll(merged[0], 2), merged[1])
        for z in range(2):
            for b in range(3):
                tile = jnp.concatenate([roll(both, 7 - 2 * v - 64 * z - 8 * b) for v in range(4)], axis=0)
                high, low = split(tile)
                row = z * 128 + b * 32
                field[bi, row : row + 32, 512:640] = high
                field[bi, 256 + row : 288 + row, 512:640] = low

    def row_block(kernel, a, c):
        return jnp.concatenate(
            [kernel[9 * a + 3 * b + c] for b in range(3)] + [jnp.zeros((32, 32), F32)], axis=1
        )

    def store_weights(wi, row, col, tile):
        high, low = split(tile)
        weights[wi, row : row + 32, col : col + 128] = high
        weights[wi, row : row + 32, 256 + col : 384 + col] = high
        weights[wi, row : row + 32, 512 + col : 640 + col] = low

    def build_weights(layer, kernel):
        for a in range(3):
            blocks = [row_block(kernel, a, c) for c in range(3)]
            flipped = jnp.concatenate(blocks + [zero32], axis=0).T
            for c in range(3):
                back = jnp.concatenate(
                    [
                        flipped[(2 - b) * 32 : (3 - b) * 32, (2 - c) * 32 : (3 - c) * 32]
                        for b in range(3)
                    ]
                    + [jnp.zeros((32, 32), F32)],
                    axis=1,
                )
                for z in range(2):
                    zp = a + z - 1
                    if 0 <= zp < 2:
                        store_weights(layer, c * 64 + z * 32, zp * 128, blocks[c])
                        store_weights(3 + layer, c * 64 + zp * 32, z * 128, back)

    def conv(wi, bi):
        for lo, hi in ((0, 256), (256, 512), (512, 640)):
            prod[:, lo:hi] = jnp.dot(
                weights[wi, :, 0:512], field[bi, :, lo:hi], preferred_element_type=F32
            ) + jnp.dot(weights[wi, :, 512:768], field[bi, 0:256, lo:hi], preferred_element_type=F32)
        out = []
        for z in range(2):
            row = z * 32
            edge = jnp.where(
                lane32 % 8 == 0, prod[row : row + 32, 512:640], prod[128 + row : 160 + row, 512:640]
            )
            tiles = []
            for x in range(4):
                col = x * 128
                at_edge = roll(edge, -8 * x)
                before = roll(prod[row : row + 32, col : col + 128], 1)
                after = roll(prod[128 + row : 160 + row, col : col + 128], -1)
                tiles.append(
                    prod[64 + row : 96 + row, col : col + 128]
                    + jnp.where(lane32 == 0, at_edge, before)
                    + jnp.where(lane32 == 127, at_edge, after)
                )
            out.append(tiles)
        return out

    def store_h(c, z, col, tile):
        high, low = split(tile)
        row = c * 64 + z * 32
        hmat[row : row + 32, col : col + 128] = high
        hmat[192 + row : 224 + row, col : col + 128] = low

    def kernel_grad(layer, bi, tiles, packed):
        for z in range(2):
            for x in range(4):
                col = x * 128
                store_h(0, z, col, jnp.where(lane32 == 127, 0.0, roll(tiles[z][x], -1)))
                store_h(1, z, col, tiles[z][x])
                store_h(2, z, col, jnp.where(lane32 == 0, 0.0, roll(tiles[z][x], 1)))
            store_h(0, z, 512, jnp.where(lane32 % 8 == 0, packed[z], 0.0))
            store_h(1, z, 512, zero32)
            store_h(2, z, 512, jnp.where(lane32 % 8 == 7, packed[z], 0.0))
        contract = (((1,), (1,)), ((), ()))
        main = lax.dot_general(hmat[...], field[bi, 0:256, :], contract, preferred_element_type=F32)
        rest = lax.dot_general(hmat[0:192, :], field[bi, 256:512, :], contract, preferred_element_type=F32)
        total = main[0:192] + main[192:384] + rest
        blocks = []
        for c in range(3):
            top, low = total[c * 64 : c * 64 + 32], total[c * 64 + 32 : c * 64 + 64]
            blocks += [low[:, 0:128], top[:, 0:128] + low[:, 128:256], top[:, 128:256]]
        for j in range(8):
            block = blocks[j]
            if j < 3:
                block = jnp.where(lane32 >= 96, roll(blocks[8], 96 - 32 * j), block)
            part[layer, 4 * j : 4 * j + 4] = block.reshape(4, 8, 128)

    def group_copy(src, dst, send_sem, recv_sem, device):
        return pltpu.make_async_remote_copy(
            src_ref=src, dst_ref=dst, send_sem=send_sem, recv_sem=recv_sem, device_id=device, device_id_type=MESH
        )

    def rs_start(layer):
        for device, m in peers:
            group_copy(
                part.at[layer, pl.ds(m * per, per)], rs_recv.at[layer, pl.ds(me * per, per)],
                rs_send_sem.at[layer], rs_recv_sem.at[layer], device,
            ).start()
        rs_recv[layer, pl.ds(me * per, per)] = part[layer, pl.ds(me * per, per)]

    def rs_wait(layer):
        count = (members - 1) * per
        return group_copy(
            part.at[layer, pl.ds(0, count)], rs_recv.at[layer, pl.ds(0, count)],
            rs_send_sem.at[layer], rs_recv_sem.at[layer], near(1, 0),
        )

    def z_start(layer):
        rs_wait(layer).wait_recv()
        total = rs_recv[layer, 0:per]
        for m in range(1, members):
            total = total + rs_recv[layer, m * per : m * per + per]
        z_recv[layer, my_z] = total

        for device in z_peers:
            group_copy(
                z_recv.at[layer, my_z], z_recv.at[layer, my_z], z_send_sem.at[layer], z_recv_sem.at[layer], device
            ).start()

    def z_wait(layer):
        return group_copy(
            z_recv.at[layer, pl.ds(0, zn - 1)], z_recv.at[layer, pl.ds(0, zn - 1)],
            z_send_sem.at[layer], z_recv_sem.at[layer], near(1, 0),
        )

    def ag_start(layer):
        z_wait(layer).wait_recv()
        total = z_recv[layer, 0]
        for k in range(1, zn):
            total = total + z_recv[layer, k]
        mine = pl.ds(me * per, per)
        ag_recv[layer, mine] = total

        for device, _ in peers:
            group_copy(
                ag_recv.at[layer, mine], ag_recv.at[layer, mine], ag_send_sem.at[layer], ag_recv_sem.at[layer], device
            ).start()

    def ag_wait(layer):
        count = pl.ds(0, (members - 1) * per)
        return group_copy(
            ag_recv.at[layer, count], ag_recv.at[layer, count],
            ag_send_sem.at[layer], ag_recv_sem.at[layer], near(1, 0),
        )

    def finish(layer):
        ag_wait(layer).wait_recv()
        red_ref[layer] = ag_recv[layer]

    def sequence():
        loads[0].wait()
        tiles = load_tiles(x3)
        fill_send(0, tiles, edge_columns(tiles))
        pl.semaphore_wait(barrier, len(greeted))
        start_halo(0)
        fill_own(0, tiles)
        for f, ref, at in ((1, x2, 3), (2, x1, 4)):
            loads[at].wait()
            tiles = load_tiles(ref)
            fill_send(f, tiles, edge_columns(tiles))
            start_halo(f)
            fill_own(f, tiles)
        loads[1].wait()
        build_weights(0, k3)
        loads[2].wait()
        loads[5].wait()
        loads[6].wait()
        grad = load_tiles(cot)

        for layer in range(3):
            if layer == 0:
                halo_wait(0)
                fill_halo(0, 0)
                pre = conv(0, 0)
                mult = [[gelu_slope(pre[z][x]) for x in range(4)] for z in range(2)]
            else:
                mult = [
                    [slope[layer - 1, (z * 4 + x) * 32 : (z * 4 + x) * 32 + 32, :] for x in range(4)] for z in range(2)
                ]
            h = [[grad[z][x] * mult[z][x] for x in range(4)] for z in range(2)]
            packed = edge_columns(h)
            fill_send(3 + layer, h, packed)
            start_halo(3 + layer)
            fill_own(3, h)
            kernel_grad(layer, layer, h, packed)
            rs_start(layer)
            if layer < 2:
                build_weights(layer + 1, (k2, k1)[layer])
                halo_wait(layer + 1)
                fill_halo(layer + 1, layer + 1)
                pre = conv(layer + 1, layer + 1)
                for z in range(2):
                    for x in range(4):
                        at = (z * 4 + x) * 32
                        slope[layer, at : at + 32, :] = gelu_slope(pre[z][x])
            halo_wait(3 + layer)
            fill_halo(3, 3 + layer)
            grad = conv(3 + layer, 3)
            if layer == 1:
                z_start(0)
        for z in range(2):
            for x in range(4):
                gin_ref[pl.ds(z * 4 + x, 32, stride=8), :] = grad[z][x]
        z_start(1)
        ag_start(0)
        z_start(2)
        ag_start(1)
        finish(0)
        ag_start(2)
        finish(1)
        finish(2)
        for f in range(6):
            whole_halo(f).wait_send()
        for layer in range(3):
            rs_wait(layer).wait_send()
            z_wait(layer).wait_send()
            ag_wait(layer).wait_send()

    sequence()


def unpack_kernel(factor, gin_in, red_ref, gin_out, *refs):
    outs, held, sem = refs[0:3], refs[3:6], refs[6]
    copies = [pltpu.make_async_copy(gin_in, gin_out, sem.at[3])]
    copies[0].start()
    for layer in range(3):
        for a in range(3):
            for b in range(3):
                for c in range(3):
                    j = c * 3 + a
                    row, col = (j * 32, b * 32) if j < 8 else (b * 32, 96)
                    held[layer][9 * a + 3 * b + c] = red_ref[layer, row : row + 32, col : col + 32] * factor
        copies.append(pltpu.make_async_copy(held[layer], outs[layer], sem.at[layer]))
        copies[-1].start()
    for copy in copies:
        copy.wait()


def per_device(dims, factor, x1, x2, x3, cot, k1, k2, k3):
    flat = [v.reshape(256, 128) for v in (x3, cot, x2, x1)]
    vmem = pl.BlockSpec(memory_space=pltpu.VMEM)
    hbm = pl.BlockSpec(memory_space=pltpu.HBM)
    members = dims[3] * 2 * dims[1]
    per = 32 // members
    dma = pltpu.SemaphoreType.DMA
    gin, red = pl.pallas_call(
        functools.partial(step_kernel, dims),
        out_shape=(jax.ShapeDtypeStruct((256, 128), F32), jax.ShapeDtypeStruct((3, 32, 8, 128), F32)),
        in_specs=[hbm] * 7,
        out_specs=(vmem, vmem),
        scratch_shapes=[pltpu.VMEM((256, 128), F32)] * 4
        + [pltpu.VMEM((27, 32, 32), F32)] * 3
        + [
            pltpu.VMEM((6, 136, 128), F32),
            pltpu.VMEM((6, 176, 128), F32),
            pltpu.VMEM((4, 512, 640), BF16),
            pltpu.VMEM((6, 192, 768), BF16),
            pltpu.VMEM((384, 640), BF16),
            pltpu.VMEM((192, 640), F32),
            pltpu.VMEM((2, 256, 128), F32),
            pltpu.VMEM((3, 32, 8, 128), F32),
            pltpu.VMEM((3, 32, 8, 128), F32),
            pltpu.VMEM((3, dims[2], per, 8, 128), F32),
            pltpu.VMEM((3, 32, 8, 128), F32),
            dma((7,)), dma((6,)), dma((6,)), dma((3,)), dma((3,)), dma((3,)), dma((3,)), dma((3,)), dma((3,)),
        ],
        compiler_params=pltpu.CompilerParams(
            collective_id=0, has_side_effects=True, vmem_limit_bytes=40 * 1024 * 1024
        ),
        name="step",
    )(*[pltpu.with_memory_space_constraint(v, pltpu.HBM) for v in (*flat, k3, k2, k1)])
    shape = jax.ShapeDtypeStruct(k1.shape, F32)
    gin, out3, out2, out1 = pl.pallas_call(
        functools.partial(unpack_kernel, factor),
        out_shape=(jax.ShapeDtypeStruct((256, 128), F32), shape, shape, shape),
        in_specs=[vmem] * 2,
        out_specs=(hbm,) * 4,
        scratch_shapes=[pltpu.VMEM(k1.shape, F32)] * 3 + [dma((4,))],
        compiler_params=pltpu.CompilerParams(vmem_limit_bytes=8 * 1024 * 1024),
        name="unpack",
    )(gin, red.reshape(3, 256, 128))
    return gin.reshape(x1.shape), out1, out2, out3


def solution(mesh):
    gxn, gyn = mesh.shape["gx"], mesh.shape["gy"]
    zn = min(8, gxn // 2)
    dims = (gxn, gyn, zn, gxn // (2 * zn))
    factor = 1.0 / math.sqrt(2 * 4 * 128 * gxn * gyn)
    placed = P(None, None, "gx", "gy")
    return jax.shard_map(
        functools.partial(per_device, dims, factor),
        mesh=mesh,
        in_specs=(placed,) * 4 + (P(),) * 3,
        out_specs=(placed, P(), P(), P()),
        check_vma=False,
    )
```

```python
import functools
import math

import jax
import jax.numpy as jnp
from jax import lax
from jax.experimental import pallas as pl
from jax.experimental.pallas import tpu as pltpu
from jax.sharding import PartitionSpec as P

MESH = pl.DeviceIdType.MESH
F32, BF16 = jnp.float32, jnp.bfloat16
INV_ROOT_TWO = 0.7071067811865476
INV_ROOT_TWO_PI = 0.3989422804014327
SIDES = ((-1, -1), (0, -1), (1, -1), (-1, 1), (0, 1), (1, 1))


def gelu_slope(value):
    normal_cdf = 0.5 * (1.0 + lax.erf(value * INV_ROOT_TWO))
    density = jnp.exp(-0.5 * value * value) * INV_ROOT_TWO_PI
    return normal_cdf + value * density


def split(value):
    high = value.astype(BF16)
    low = (value - high.astype(F32)).astype(BF16)
    return high, low


def roll(value, shift):
    shift = shift % 128
    return value if shift == 0 else pltpu.roll(value, shift, 1)


def lanes(rows):
    return lax.broadcasted_iota(jnp.int32, (rows, 128), 1)


def step_kernel(
    dims, x3_in, cot_in, x2_in, x1_in, k3_in, k2_in, k1_in,
    gin_ref, red_ref,
    x3, cot, x2, x1, k3, k2, k1,
    send, recv, field, weights, hmat, prod, slope,
    part, rs_recv, z_recv, ag_recv,
    load_sem, halo_send, halo_recv, rs_send_sem, rs_recv_sem, z_send_sem, z_recv_sem, ag_send_sem, ag_recv_sem,
):
    gxn, gyn, zn, ylo = dims
    members = ylo * 2 * gyn
    per = 32 // members
    gx, gy = lax.axis_index("gx"), lax.axis_index("gy")
    core, my_z, my_y = lax.rem(gx, 2), lax.rem(lax.div(gx, 2), zn), lax.div(gx, 2 * zn)
    me = (my_y * 2 + core) * gyn + gy

    xs = min(4, gyn)
    yhi = gyn // xs
    my_x, my_yhi = lax.rem(gy, xs), lax.div(gy, xs)
    cores = [lax.rem(core + k, 2) for k in range(2)]
    lows = [lax.rem(my_y + k, ylo) for k in range(ylo)]
    highs = [lax.rem(my_yhi + k, yhi) for k in range(yhi)]
    columns = [lax.rem(my_x + k, xs) for k in range(xs)]
    order = []
    for kc in range(2):
        for kl in range(ylo):
            for kh in range(yhi):
                for kx in range(xs):
                    hops = min(kx, xs - kx) + (1 if kl else 2 * kh)
                    order.append((-hops, kc, kl, kh, kx))
    peers = []
    for _, kc, kl, kh, kx in sorted(order):
        if kc or kl or kh or kx:
            spot = highs[kh] * xs + columns[kx]
            line = lows[kl] * 2 + cores[kc]
            at = lows[kl] * (2 * zn) + my_z * 2 + cores[kc]
            peers.append(((at, spot), line * gyn + spot))
    z_order = sorted(range(1, zn), key=lambda k: -min(k, zn - k))
    z_peers = [(my_y * (2 * zn) + lax.rem(my_z + k, zn) * 2 + core, gy) for k in z_order]

    def near(n, side):
        return (lax.rem(gx + n + gxn, gxn), lax.rem(gy + side + gyn, gyn))

    loads = []
    for i, (src, dst) in enumerate(
        ((x3_in, x3), (k3_in, k3), (cot_in, cot), (x2_in, x2), (x1_in, x1), (k2_in, k2), (k1_in, k1))
    ):
        copy = pltpu.make_async_copy(src, dst, load_sem.at[i])
        copy.start()
        loads.append(copy)

    barrier = pltpu.get_barrier_semaphore()
    around = [near(n, s) for n, s in SIDES] + [near(-1, 0), near(1, 0)]
    greeted = z_peers + [device for device, _ in peers] + around
    for device in greeted:
        pl.semaphore_signal(barrier, inc=1, device_id=device, device_id_type=MESH)

    up = (gx > 0).astype(F32)
    down = (gx < gxn - 1).astype(F32)
    left = (gy > 0).astype(F32)
    right = (gy < gyn - 1).astype(F32)
    lane8, lane32 = lanes(8), lanes(32)
    zero32 = jnp.zeros((32, 128), F32)

    for bi in range(4):
        for part_row in (0, 256):
            for z in range(2):
                base = part_row + z * 128 + 96
                field[bi, base : base + 32, :] = jnp.zeros((32, 640), BF16)

    def load_tiles(ref):
        return [[ref[pl.ds(z * 4 + x, 32, stride=8), :] for x in range(4)] for z in range(2)]

    def edge_columns(tiles):
        packed = []
        for z in range(2):
            total = zero32
            for x in range(4):
                keep = (lane32 == 8 * x) | (lane32 == (8 * x - 1) % 128)
                total = jnp.where(keep, roll(tiles[z][x], 8 * x), total)
            packed.append(total)
        return packed

    def fill_send(f, tiles, packed):
        for z in range(2):
            send[f, z * 32 : z * 32 + 32, :] = tiles[z][0]
            send[f, 64 + z * 32 : 96 + z * 32, :] = tiles[z][3]
        squeezed = None
        for z in range(2):
            for v in range(4):
                term = roll(packed[z][8 * v : 8 * v + 8], 2 * v + 64 * z)
                squeezed = term if squeezed is None else squeezed + term
        send[f, 128:136, :] = squeezed

    def fill_own(bi, tiles):
        for z in range(2):
            for x_in in range(4):
                high, low = split(tiles[z][x_in])
                for b in range(3):
                    x = x_in + 1 - b
                    if 0 <= x < 4:
                        row, col = z * 128 + b * 32, x * 128
                        field[bi, row : row + 32, col : col + 128] = high
                        field[bi, 256 + row : 288 + row, col : col + 128] = low

    def halo_copies(f):
        copies = []

        def add(lo, hi, at, device):
            copies.append(
                pltpu.make_async_remote_copy(
                    src_ref=send.at[f, pl.ds(lo, hi - lo)],
                    dst_ref=recv.at[f, pl.ds(at, hi - lo)],
                    send_sem=halo_send.at[f],
                    recv_sem=halo_recv.at[f],
                    device_id=device,
                    device_id_type=MESH,
                )
            )

        for k, (n, s) in enumerate(SIDES):
            add(128, 136, 128 + 8 * k, near(-n, -s))
        add(64, 128, 0, near(1, 0))
        add(0, 64, 64, near(-1, 0))
        return copies

    def start_halo(f):
        for copy in halo_copies(f):
            copy.start()

    def whole_halo(f):
        return pltpu.make_async_remote_copy(
            src_ref=recv.at[f], dst_ref=recv.at[f], send_sem=halo_send.at[f], recv_sem=halo_recv.at[f],
            device_id=near(1, 0), device_id_type=MESH,
        )

    def halo_wait(f):
        whole_halo(f).wait_recv()

    def fill_halo(bi, f):
        for z in range(2):
            for at, b, x, ok in ((0, 0, 0, up), (64, 2, 3, down)):
                high, low = split(recv[f, at + z * 32 : at + z * 32 + 32, :] * ok)
                row, col = z * 128 + b * 32, x * 128
                field[bi, row : row + 32, col : col + 128] = high
                field[bi, 256 + row : 288 + row, col : col + 128] = low
        first = ((lane8 & 63) >= 55) & ((lane8 & 63) <= 62)
        last = ((lane8 & 63) >= 31) & ((lane8 & 63) <= 38)
        merged = []
        for k, ok in ((0, left), (3, right)):
            tile = [recv[f, 128 + 8 * (k + j) : 136 + 8 * (k + j), :] for j in range(3)]
            total = tile[1]
            total = total + jnp.where(first, roll(tile[0], 96), 0.0) * up
            total = total + jnp.where(last, roll(tile[2], 32), 0.0) * down
            merged.append(total * ok)
        both = jnp.where(lane8 % 2 == 1, roll(merged[0], 2), merged[1])
        for z in range(2):
            for b in range(3):
                tile = jnp.concatenate([roll(both, 7 - 2 * v - 64 * z - 8 * b) for v in range(4)], axis=0)
                high, low = split(tile)
                row = z * 128 + b * 32
                field[bi, row : row + 32, 512:640] = high
                field[bi, 256 + row : 288 + row, 512:640] = low

    def row_block(kernel, a, c):
        return jnp.concatenate(
            [kernel[9 * a + 3 * b + c] for b in range(3)] + [jnp.zeros((32, 32), F32)], axis=1
        )

    def store_weights(wi, row, col, tile):
        high, low = split(tile)
        weights[wi, row : row + 32, col : col + 128] = high
        weights[wi, row : row + 32, 256 + col : 384 + col] = high
        weights[wi, row : row + 32, 512 + col : 640 + col] = low

    def build_weights(layer, kernel):
        for a in range(3):
            blocks = [row_block(kernel, a, c) for c in range(3)]
            flipped = jnp.concatenate(blocks + [zero32], axis=0).T
            for c in range(3):
                back = jnp.concatenate(
                    [
                        flipped[(2 - b) * 32 : (3 - b) * 32, (2 - c) * 32 : (3 - c) * 32]
                        for b in range(3)
                    ]
                    + [jnp.zeros((32, 32), F32)],
                    axis=1,
                )
                for z in range(2):
                    zp = a + z - 1
                    if 0 <= zp < 2:
                        store_weights(layer, c * 64 + z * 32, zp * 128, blocks[c])
                        store_weights(3 + layer, c * 64 + zp * 32, z * 128, back)

    def conv(wi, bi):
        for lo, hi in ((0, 256), (256, 512), (512, 640)):
            prod[:, lo:hi] = jnp.dot(
                weights[wi, :, 0:512], field[bi, :, lo:hi], preferred_element_type=F32
            ) + jnp.dot(weights[wi, :, 512:768], field[bi, 0:256, lo:hi], preferred_element_type=F32)
        out = []
        for z in range(2):
            row = z * 32
            edge = jnp.where(
                lane32 % 8 == 0, prod[row : row + 32, 512:640], prod[128 + row : 160 + row, 512:640]
            )
            tiles = []
            for x in range(4):
                col = x * 128
                at_edge = roll(edge, -8 * x)
                before = roll(prod[row : row + 32, col : col + 128], 1)
                after = roll(prod[128 + row : 160 + row, col : col + 128], -1)
                tiles.append(
                    prod[64 + row : 96 + row, col : col + 128]
                    + jnp.where(lane32 == 0, at_edge, before)
                    + jnp.where(lane32 == 127, at_edge, after)
                )
            out.append(tiles)
        return out

    def store_h(c, z, col, tile):
        high, low = split(tile)
        row = c * 64 + z * 32
        hmat[row : row + 32, col : col + 128] = high
        hmat[192 + row : 224 + row, col : col + 128] = low

    def kernel_grad(layer, bi, tiles, packed):
        for z in range(2):
            for x in range(4):
                col = x * 128
                store_h(0, z, col, jnp.where(lane32 == 127, 0.0, roll(tiles[z][x], -1)))
                store_h(1, z, col, tiles[z][x])
                store_h(2, z, col, jnp.where(lane32 == 0, 0.0, roll(tiles[z][x], 1)))
            store_h(0, z, 512, jnp.where(lane32 % 8 == 0, packed[z], 0.0))
            store_h(1, z, 512, zero32)
            store_h(2, z, 512, jnp.where(lane32 % 8 == 7, packed[z], 0.0))
        contract = (((1,), (1,)), ((), ()))
        main = lax.dot_general(hmat[...], field[bi, 0:256, :], contract, preferred_element_type=F32)
        rest = lax.dot_general(hmat[0:192, :], field[bi, 256:512, :], contract, preferred_element_type=F32)
        total = main[0:192] + main[192:384] + rest
        blocks = []
        for c in range(3):
            top, low = total[c * 64 : c * 64 + 32], total[c * 64 + 32 : c * 64 + 64]
            blocks += [low[:, 0:128], top[:, 0:128] + low[:, 128:256], top[:, 128:256]]
        for j in range(8):
            block = blocks[j]
            if j < 3:
                block = jnp.where(lane32 >= 96, roll(blocks[8], 96 - 32 * j), block)
            part[layer, 4 * j : 4 * j + 4] = block.reshape(4, 8, 128)

    def group_copy(src, dst, send_sem, recv_sem, device):
        return pltpu.make_async_remote_copy(
            src_ref=src, dst_ref=dst, send_sem=send_sem, recv_sem=recv_sem, device_id=device, device_id_type=MESH
        )

    def rs_start(layer):
        for device, m in peers:
            group_copy(
                part.at[layer, pl.ds(m * per, per)], rs_recv.at[layer, pl.ds(me * per, per)],
                rs_send_sem.at[layer], rs_recv_sem.at[layer], device,
            ).start()
        rs_recv[layer, pl.ds(me * per, per)] = part[layer, pl.ds(me * per, per)]

    def rs_wait(layer):
        count = (members - 1) * per
        return group_copy(
            part.at[layer, pl.ds(0, count)], rs_recv.at[layer, pl.ds(0, count)],
            rs_send_sem.at[layer], rs_recv_sem.at[layer], near(1, 0),
        )

    def z_start(layer):
        rs_wait(layer).wait_recv()
        total = rs_recv[layer, 0:per]
        for m in range(1, members):
            total = total + rs_recv[layer, m * per : m * per + per]
        z_recv[layer, my_z] = total

        for device in z_peers:
            group_copy(
                z_recv.at[layer, my_z], z_recv.at[layer, my_z], z_send_sem.at[layer], z_recv_sem.at[layer], device
            ).start()

    def z_wait(layer):
        return group_copy(
            z_recv.at[layer, pl.ds(0, zn - 1)], z_recv.at[layer, pl.ds(0, zn - 1)],
            z_send_sem.at[layer], z_recv_sem.at[layer], near(1, 0),
        )

    def ag_start(layer):
        z_wait(layer).wait_recv()
        total = z_recv[layer, 0]
        for k in range(1, zn):
            total = total + z_recv[layer, k]
        mine = pl.ds(me * per, per)
        ag_recv[layer, mine] = total

        for device, _ in peers:
            group_copy(
                ag_recv.at[layer, mine], ag_recv.at[layer, mine], ag_send_sem.at[layer], ag_recv_sem.at[layer], device
            ).start()

    def ag_wait(layer):
        count = pl.ds(0, (members - 1) * per)
        return group_copy(
            ag_recv.at[layer, count], ag_recv.at[layer, count],
            ag_send_sem.at[layer], ag_recv_sem.at[layer], near(1, 0),
        )

    def finish(layer):
        ag_wait(layer).wait_recv()
        red_ref[layer] = ag_recv[layer]

    def sequence():
        loads[0].wait()
        tiles = load_tiles(x3)
        fill_send(0, tiles, edge_columns(tiles))
        pl.semaphore_wait(barrier, len(greeted))
        start_halo(0)
        fill_own(0, tiles)
        for f, ref, at in ((1, x2, 3), (2, x1, 4)):
            loads[at].wait()
            tiles = load_tiles(ref)
            fill_send(f, tiles, edge_columns(tiles))
            start_halo(f)
            fill_own(f, tiles)
        loads[1].wait()
        build_weights(0, k3)
        loads[2].wait()
        loads[5].wait()
        loads[6].wait()
        grad = load_tiles(cot)

        for layer in range(3):
            if layer == 0:
                halo_wait(0)
                fill_halo(0, 0)
                pre = conv(0, 0)
                mult = [[gelu_slope(pre[z][x]) for x in range(4)] for z in range(2)]
            else:
                mult = [
                    [slope[layer - 1, (z * 4 + x) * 32 : (z * 4 + x) * 32 + 32, :] for x in range(4)] for z in range(2)
                ]
            h = [[grad[z][x] * mult[z][x] for x in range(4)] for z in range(2)]
            packed = edge_columns(h)
            fill_send(3 + layer, h, packed)
            start_halo(3 + layer)
            fill_own(3, h)
            kernel_grad(layer, layer, h, packed)
            rs_start(layer)
            if layer > 0:
                z_start(layer - 1)
            if layer == 2:
                ag_start(0)
            if layer < 2:
                build_weights(layer + 1, (k2, k1)[layer])
                halo_wait(layer + 1)
                fill_halo(layer + 1, layer + 1)
                pre = conv(layer + 1, layer + 1)
                for z in range(2):
                    for x in range(4):
                        at = (z * 4 + x) * 32
                        slope[layer, at : at + 32, :] = gelu_slope(pre[z][x])
            halo_wait(3 + layer)
            fill_halo(3, 3 + layer)
            grad = conv(3 + layer, 3)
        for z in range(2):
            for x in range(4):
                gin_ref[pl.ds(z * 4 + x, 32, stride=8), :] = grad[z][x]
        ag_start(1)
        z_start(2)
        finish(0)
        ag_start(2)
        finish(1)
        finish(2)
        for f in range(6):
            whole_halo(f).wait_send()
        for layer in range(3):
            rs_wait(layer).wait_send()
            z_wait(layer).wait_send()
            ag_wait(layer).wait_send()

    sequence()


def unpack_kernel(factor, gin_in, red_ref, gin_out, *refs):
    outs, held, sem = refs[0:3], refs[3:6], refs[6]
    copies = [pltpu.make_async_copy(gin_in, gin_out, sem.at[3])]
    copies[0].start()
    for layer in range(3):
        for a in range(3):
            for b in range(3):
                for c in range(3):
                    j = c * 3 + a
                    row, col = (j * 32, b * 32) if j < 8 else (b * 32, 96)
                    held[layer][9 * a + 3 * b + c] = red_ref[layer, row : row + 32, col : col + 32] * factor
        copies.append(pltpu.make_async_copy(held[layer], outs[layer], sem.at[layer]))
        copies[-1].start()
    for copy in copies:
        copy.wait()


def per_device(dims, factor, x1, x2, x3, cot, k1, k2, k3):
    flat = [v.reshape(256, 128) for v in (x3, cot, x2, x1)]
    vmem = pl.BlockSpec(memory_space=pltpu.VMEM)
    hbm = pl.BlockSpec(memory_space=pltpu.HBM)
    members = dims[3] * 2 * dims[1]
    per = 32 // members
    dma = pltpu.SemaphoreType.DMA
    gin, red = pl.pallas_call(
        functools.partial(step_kernel, dims),
        out_shape=(jax.ShapeDtypeStruct((256, 128), F32), jax.ShapeDtypeStruct((3, 32, 8, 128), F32)),
        in_specs=[hbm] * 7,
        out_specs=(vmem, vmem),
        scratch_shapes=[pltpu.VMEM((256, 128), F32)] * 4
        + [pltpu.VMEM((27, 32, 32), F32)] * 3
        + [
            pltpu.VMEM((6, 136, 128), F32),
            pltpu.VMEM((6, 176, 128), F32),
            pltpu.VMEM((4, 512, 640), BF16),
            pltpu.VMEM((6, 192, 768), BF16),
            pltpu.VMEM((384, 640), BF16),
            pltpu.VMEM((192, 640), F32),
            pltpu.VMEM((2, 256, 128), F32),
            pltpu.VMEM((3, 32, 8, 128), F32),
            pltpu.VMEM((3, 32, 8, 128), F32),
            pltpu.VMEM((3, dims[2], per, 8, 128), F32),
            pltpu.VMEM((3, 32, 8, 128), F32),
            dma((7,)), dma((6,)), dma((6,)), dma((3,)), dma((3,)), dma((3,)), dma((3,)), dma((3,)), dma((3,)),
        ],
        compiler_params=pltpu.CompilerParams(
            collective_id=0, has_side_effects=True, vmem_limit_bytes=40 * 1024 * 1024
        ),
        name="step",
    )(*[pltpu.with_memory_space_constraint(v, pltpu.HBM) for v in (*flat, k3, k2, k1)])
    shape = jax.ShapeDtypeStruct(k1.shape, F32)
    gin, out3, out2, out1 = pl.pallas_call(
        functools.partial(unpack_kernel, factor),
        out_shape=(jax.ShapeDtypeStruct((256, 128), F32), shape, shape, shape),
        in_specs=[vmem] * 2,
        out_specs=(hbm,) * 4,
        scratch_shapes=[pltpu.VMEM(k1.shape, F32)] * 3 + [dma((4,))],
        compiler_params=pltpu.CompilerParams(vmem_limit_bytes=8 * 1024 * 1024),
        name="unpack",
    )(gin, red.reshape(3, 256, 128))
    return gin.reshape(x1.shape), out1, out2, out3


def solution(mesh):
    gxn, gyn = mesh.shape["gx"], mesh.shape["gy"]
    zn = min(8, gxn // 2)
    dims = (gxn, gyn, zn, gxn // (2 * zn))
    factor = 1.0 / math.sqrt(2 * 4 * 128 * gxn * gyn)
    placed = P(None, None, "gx", "gy")
    return jax.shard_map(
        functools.partial(per_device, dims, factor),
        mesh=mesh,
        in_specs=(placed,) * 4 + (P(),) * 3,
        out_specs=(placed, P(), P(), P()),
        check_vma=False,
    )
```

```python
import functools
import math

import jax
import jax.numpy as jnp
from jax import lax
from jax.experimental import pallas as pl
from jax.experimental.pallas import tpu as pltpu
from jax.sharding import PartitionSpec as P

MESH = pl.DeviceIdType.MESH
F32, BF16 = jnp.float32, jnp.bfloat16
INV_ROOT_TWO = 0.7071067811865476
INV_ROOT_TWO_PI = 0.3989422804014327
SIDES = ((-1, -1), (0, -1), (1, -1), (-1, 1), (0, 1), (1, 1))


def gelu_slope(value):
    normal_cdf = 0.5 * (1.0 + lax.erf(value * INV_ROOT_TWO))
    density = jnp.exp(-0.5 * value * value) * INV_ROOT_TWO_PI
    return normal_cdf + value * density


def split(value):
    high = value.astype(BF16)
    low = (value - high.astype(F32)).astype(BF16)
    return high, low


def roll(value, shift):
    shift = shift % 128
    return value if shift == 0 else pltpu.roll(value, shift, 1)


def lanes(rows):
    return lax.broadcasted_iota(jnp.int32, (rows, 128), 1)


def tile_of(row):
    return row if 0 <= row < 4 else (5 - 2 * (row + 1) if row < 0 else 6 + 2 * (row - 4))


def step_kernel(
    dims, x3_in, cot_in, x2_in, x1_in, k3_in, k2_in, k1_in,
    gin_ref, red_ref,
    x3, cot, x2, x1, k3, k2, k1,
    send, recv, field, weights, hmat, prod, held,
    part, rs_recv, z_recv, ag_recv,
    load_sem, halo_send, halo_recv, rs_send_sem, rs_recv_sem, z_send_sem, z_recv_sem, ag_send_sem, ag_recv_sem,
):
    gxn, gyn, zn, ylo = dims
    members = ylo * 2 * gyn
    per = 32 // members
    gx, gy = lax.axis_index("gx"), lax.axis_index("gy")
    core, my_z, my_y = lax.rem(gx, 2), lax.rem(lax.div(gx, 2), zn), lax.div(gx, 2 * zn)
    me = (my_y * 2 + core) * gyn + gy

    xs = min(4, gyn)
    yhi = gyn // xs
    my_x, my_yhi = lax.rem(gy, xs), lax.div(gy, xs)
    cores = [lax.rem(core + k, 2) for k in range(2)]
    lows = [lax.rem(my_y + k, ylo) for k in range(ylo)]
    highs = [lax.rem(my_yhi + k, yhi) for k in range(yhi)]
    columns = [lax.rem(my_x + k, xs) for k in range(xs)]
    order = []
    for kc in range(2):
        for kl in range(ylo):
            for kh in range(yhi):
                for kx in range(xs):
                    hops = min(kx, xs - kx) + (1 if kl else 2 * kh)
                    order.append((-hops, kc, kl, kh, kx))
    peers = []
    for _, kc, kl, kh, kx in sorted(order):
        if kc or kl or kh or kx:
            spot = highs[kh] * xs + columns[kx]
            line = lows[kl] * 2 + cores[kc]
            at = lows[kl] * (2 * zn) + my_z * 2 + cores[kc]
            peers.append(((at, spot), line * gyn + spot))
    z_order = sorted(range(1, zn), key=lambda k: -min(k, zn - k))
    z_peers = [(my_y * (2 * zn) + lax.rem(my_z + k, zn) * 2 + core, gy) for k in z_order]

    def near(n, side):
        return (lax.rem(gx + n + gxn, gxn), lax.rem(gy + side + gyn, gyn))

    loads = []
    for i, (src, dst) in enumerate(
        ((x3_in, x3), (k3_in, k3), (cot_in, cot), (x2_in, x2), (x1_in, x1), (k2_in, k2), (k1_in, k1))
    ):
        copy = pltpu.make_async_copy(src, dst, load_sem.at[i])
        copy.start()
        loads.append(copy)

    barrier = pltpu.get_barrier_semaphore()
    around = [near(n, s) for n, s in SIDES] + [near(-1, 0), near(1, 0)]
    greeted = z_peers + [device for device, _ in peers] + around
    for device in greeted:
        pl.semaphore_signal(barrier, inc=1, device_id=device, device_id_type=MESH)

    up = (gx > 0).astype(F32)
    down = (gx < gxn - 1).astype(F32)
    left = (gy > 0).astype(F32)
    right = (gy < gyn - 1).astype(F32)
    lane8, lane32 = lanes(8), lanes(32)
    zero32 = jnp.zeros((32, 128), F32)

    spot8, spot32 = lane8 % 8, lane32 % 8
    outside = jnp.where(spot8 < 3, left, jnp.where(spot8 >= 5, right, 1.0))
    outside = outside * jnp.where(lane8 < 24, up, jnp.where(lane8 >= 56, down, 1.0))
    outside = jnp.concatenate([outside] * 4, axis=0)

    def clear_padding():
        for bi in range(6):
            width = 128 * (9, 7, 5, 7, 5, 5)[bi]
            for base in (96, 224, 352, 480):
                field[bi, base : base + 32, 0:width] = jnp.zeros((32, width), BF16)

    def load_tiles(ref):
        return [{x: ref[pl.ds(z * 4 + x, 32, stride=8), :] for x in range(4)} for z in range(2)]

    def edge_columns(tiles):
        packed = []
        for z in range(2):
            total = zero32
            for row, tile in tiles[z].items():
                base = 8 * (row + 3)
                total = jnp.where((lane32 >= base + 2) & (lane32 < base + 8), roll(tile, base + 5), total)
            packed.append(total)
        return packed

    def fill_send(f, tiles, packed):
        for z in range(2):
            squeezed = None
            for v in range(4):
                term = roll(packed[z][8 * v : 8 * v + 8], 32 * v - 24)
                squeezed = term if squeezed is None else squeezed + term
            send[f, 256 + 8 * z : 264 + 8 * z, :] = squeezed
        for z in range(2):
            for x in range(4):
                send[f, x * 64 + z * 32 : x * 64 + z * 32 + 32, :] = tiles[z][x]

    def fill_rows(bi, extent, tiles):
        for z in range(2):
            for row_in, tile in tiles[z].items():
                high, low = split(tile)
                for b in range(3):
                    row_out = row_in + 1 - b
                    if -extent <= row_out < 4 + extent:
                        row, col = z * 128 + b * 32, tile_of(row_out) * 128
                        field[bi, row : row + 32, col : col + 128] = high
                        field[bi, 256 + row : 288 + row, col : col + 128] = low

    def fill_edges(bi, edges):
        for z in range(2):
            for b in range(3):
                high, low = split(roll(edges[z], 8 - 8 * b))
                row = z * 128 + b * 32
                field[bi, row : row + 32, 512:640] = high
                field[bi, 256 + row : 288 + row, 512:640] = low

    def own_edges(packed, other):
        return [
            jnp.where(spot32 == 4, packed[z], jnp.where(spot32 == 3, roll(packed[z], -2), other[z]))
            for z in range(2)
        ]

    depth = (3, 2, 2, 1, 1)

    def start_halo(f):
        d = depth[f] * 64

        def go(src, dst, rows, device):
            pltpu.make_async_remote_copy(
                src_ref=send.at[f, pl.ds(src, rows)],
                dst_ref=recv.at[f, pl.ds(dst, rows)],
                send_sem=halo_send.at[f],
                recv_sem=halo_recv.at[f],
                device_id=device,
                device_id_type=MESH,
            ).start()

        for k in (0, 2, 3, 5, 1, 4):
            go(256, 2 * d + 16 * k, 16, near(-SIDES[k][0], -SIDES[k][1]))
        go(256 - d, 0, d, near(1, 0))
        go(0, d, d, near(-1, 0))

    def whole_halo(f):
        ref = recv.at[f, pl.ds(0, 128 * depth[f] + 96)]
        return pltpu.make_async_remote_copy(
            src_ref=ref, dst_ref=ref, send_sem=halo_send.at[f], recv_sem=halo_recv.at[f],
            device_id=near(1, 0), device_id_type=MESH,
        )

    def halo_rows(f):
        d = depth[f]
        rows = [{}, {}]
        for z in range(2):
            for i in range(d):
                at = i * 64 + z * 32
                rows[z][i - d] = recv[f, at : at + 32, :] * up
                rows[z][4 + i] = recv[f, d * 64 + at : d * 64 + at + 32, :] * down
        return rows

    def halo_edges(f):
        base = 128 * depth[f]
        edges = []
        for z in range(2):
            merged = []
            for j, ok in ((0, up), (1, None), (2, down)):
                at = base + 16 * j + 8 * z
                near_left, near_right = recv[f, at : at + 8, :], recv[f, at + 48 : at + 56, :]
                tile = jnp.where(spot8 < 3, roll(near_left, -2) * left, jnp.where(spot8 >= 5, near_right * right, 0.0))
                merged.append(tile if ok is None else tile * ok)
            tiles = []
            for v in range(4):
                tile = jnp.where(lane8 < 24, roll(merged[0], -8 - 32 * v), roll(merged[1], 24 - 32 * v))
                tile = jnp.where(lane8 >= 56, roll(merged[2], 56 - 32 * v), tile)
                tiles.append(jnp.where(lane8 < 88, tile, 0.0))
            edges.append(jnp.concatenate(tiles, axis=0))
        return edges

    def row_block(kernel, a, c):
        return jnp.concatenate(
            [kernel[9 * a + 3 * b + c] for b in range(3)] + [jnp.zeros((32, 32), F32)], axis=1
        )

    def store_weights(wi, row, col, tile):
        high, low = split(tile)
        weights[wi, row : row + 32, col : col + 128] = high
        weights[wi, row : row + 32, 256 + col : 384 + col] = high
        weights[wi, row : row + 32, 512 + col : 640 + col] = low

    def build_weights(layer, kernel):
        for a in range(3):
            blocks = [row_block(kernel, a, c) for c in range(3)]
            flipped = jnp.concatenate(blocks + [zero32], axis=0).T
            for c in range(3):
                back = jnp.concatenate(
                    [
                        flipped[(2 - b) * 32 : (3 - b) * 32, (2 - c) * 32 : (3 - c) * 32]
                        for b in range(3)
                    ]
                    + [jnp.zeros((32, 32), F32)],
                    axis=1,
                )
                for z in range(2):
                    zp = a + z - 1
                    if 0 <= zp < 2:
                        store_weights(layer, c * 64 + z * 32, zp * 128, blocks[c])
                        store_weights(3 + layer, c * 64 + zp * 32, z * 128, back)

    def conv(wi, bi, extent):
        width = 128 * (5 + 2 * extent)
        for lo in range(0, width, 256):
            hi = min(lo + 256, width)
            prod[:, lo:hi] = jnp.dot(
                weights[wi, :, 0:512], field[bi, :, lo:hi], preferred_element_type=F32
            ) + jnp.dot(weights[wi, :, 512:768], field[bi, 0:256, lo:hi], preferred_element_type=F32)
        out, edges = [], []
        for z in range(2):
            row = z * 32
            p0, p1, p2 = (prod[c * 64 + row : c * 64 + row + 32, 512:640] for c in range(3))
            edge = jnp.where(spot32 == 2, p0, roll(p2, -4))
            if extent:
                edges.append(p1 + roll(p0, 1) + roll(p2, -1))
            tiles = {}
            for x in range(-extent, 4 + extent):
                col = tile_of(x) * 128
                at_edge = roll(edge, -8 * (x + 3) - 2)
                before = roll(prod[row : row + 32, col : col + 128], 1)
                after = roll(prod[128 + row : 160 + row, col : col + 128], -1)
                tiles[x] = (
                    prod[64 + row : 96 + row, col : col + 128]
                    + jnp.where(lane32 == 0, at_edge, before)
                    + jnp.where(lane32 == 127, at_edge, after)
                )
            out.append(tiles)
        return out, edges

    def store_h(c, z, col, tile):
        high, low = split(tile)
        row = c * 64 + z * 32
        hmat[row : row + 32, col : col + 128] = high
        hmat[192 + row : 224 + row, col : col + 128] = low

    def keep_h(layer, tiles, packed):
        for z in range(2):
            for x in range(4):
                at = (z * 5 + x) * 32
                held[layer, at : at + 32, :] = tiles[z][x]
            held[layer, z * 160 + 128 : z * 160 + 160, :] = packed[z]

    def kernel_grad(layer):
        bi = layer
        own = (lane32 >= 24) & (lane32 < 56)
        for z in range(2):
            for x in range(4):
                col, at = x * 128, (z * 5 + x) * 32
                tile = held[layer, at : at + 32, :]
                store_h(0, z, col, jnp.where(lane32 == 127, 0.0, roll(tile, -1)))
                store_h(1, z, col, tile)
                store_h(2, z, col, jnp.where(lane32 == 0, 0.0, roll(tile, 1)))
            packed = held[layer, z * 160 + 128 : z * 160 + 160, :]
            store_h(0, z, 512, jnp.where(own & (spot32 == 2), roll(packed, -3), 0.0))
            store_h(1, z, 512, zero32)
            store_h(2, z, 512, jnp.where(own & (spot32 == 5), roll(packed, 1), 0.0))
        contract = (((1,), (1,)), ((), ()))
        main = lax.dot_general(hmat[...], field[bi, 0:256, 0:640], contract, preferred_element_type=F32)
        rest = lax.dot_general(hmat[0:192, :], field[bi, 256:512, 0:640], contract, preferred_element_type=F32)
        total = main[0:192] + main[192:384] + rest
        blocks = []
        for c in range(3):
            top, low = total[c * 64 : c * 64 + 32], total[c * 64 + 32 : c * 64 + 64]
            blocks += [low[:, 0:128], top[:, 0:128] + low[:, 128:256], top[:, 128:256]]
        for j in range(8):
            block = blocks[j]
            if j < 3:
                block = jnp.where(lane32 >= 96, roll(blocks[8], 96 - 32 * j), block)
            part[layer, 4 * j : 4 * j + 4] = block.reshape(4, 8, 128)

    def group_copy(src, dst, send_sem, recv_sem, device):
        return pltpu.make_async_remote_copy(
            src_ref=src, dst_ref=dst, send_sem=send_sem, recv_sem=recv_sem, device_id=device, device_id_type=MESH
        )

    def rs_start(layer):
        for device, m in peers:
            group_copy(
                part.at[layer, pl.ds(m * per, per)], rs_recv.at[layer, pl.ds(me * per, per)],
                rs_send_sem.at[layer], rs_recv_sem.at[layer], device,
            ).start()
        rs_recv[layer, pl.ds(me * per, per)] = part[layer, pl.ds(me * per, per)]

    def rs_wait(layer):
        count = (members - 1) * per
        return group_copy(
            part.at[layer, pl.ds(0, count)], rs_recv.at[layer, pl.ds(0, count)],
            rs_send_sem.at[layer], rs_recv_sem.at[layer], near(1, 0),
        )

    def z_start(layer):
        rs_wait(layer).wait_recv()
        total = rs_recv[layer, 0:per]
        for m in range(1, members):
            total = total + rs_recv[layer, m * per : m * per + per]
        z_recv[layer, my_z] = total

        for device in z_peers:
            group_copy(
                z_recv.at[layer, my_z], z_recv.at[layer, my_z], z_send_sem.at[layer], z_recv_sem.at[layer], device
            ).start()

    def z_wait(layer):
        return group_copy(
            z_recv.at[layer, pl.ds(0, zn - 1)], z_recv.at[layer, pl.ds(0, zn - 1)],
            z_send_sem.at[layer], z_recv_sem.at[layer], near(1, 0),
        )

    def ag_start(layer):
        z_wait(layer).wait_recv()
        total = z_recv[layer, 0]
        for k in range(1, zn):
            total = total + z_recv[layer, k]
        mine = pl.ds(me * per, per)
        ag_recv[layer, mine] = total

        for device, _ in peers:
            group_copy(
                ag_recv.at[layer, mine], ag_recv.at[layer, mine], ag_send_sem.at[layer], ag_recv_sem.at[layer], device
            ).start()

    def ag_wait(layer):
        count = pl.ds(0, (members - 1) * per)
        return group_copy(
            ag_recv.at[layer, count], ag_recv.at[layer, count],
            ag_send_sem.at[layer], ag_recv_sem.at[layer], near(1, 0),
        )

    def finish(layer):
        ag_wait(layer).wait_recv()
        red_ref[layer] = ag_recv[layer]

    def sequence():
        loads[0].wait()
        tiles3 = load_tiles(x3)
        packed3 = edge_columns(tiles3)
        fill_send(0, tiles3, packed3)
        pl.semaphore_wait(barrier, len(greeted))
        start_halo(0)
        zero = [zero32, zero32]
        for f, ref, at in ((1, cot, 2), (2, x2, 3), (3, x1, 4)):
            loads[at].wait()
            tiles = load_tiles(ref)
            packed = edge_columns(tiles)
            fill_send(f, tiles, packed)
            start_halo(f)
            if f > 1:
                fill_rows(f - 1, 3 - f, tiles)
        clear_padding()
        fill_rows(0, 2, tiles3)
        for at, kernel, layer in ((1, k3, 0), (5, k2, 1), (6, k1, 2)):
            loads[at].wait()
            build_weights(layer, kernel)

        def forward(layer, f, extent, ref):
            near_packed = edge_columns(load_tiles(ref)) if extent else zero
            whole_halo(f).wait_recv()
            rows, edges = halo_rows(f), halo_edges(f)
            fill_rows(layer, extent, rows)
            if extent:
                far_packed = edge_columns(rows)
                edges = own_edges([near_packed[z] + far_packed[z] for z in range(2)], edges)
            fill_edges(layer, edges)
            return conv(layer, layer, extent)

        pre, pre_edge = forward(0, 0, 2, x3)
        whole_halo(1).wait_recv()
        grad, far = load_tiles(cot), halo_rows(1)
        h = []
        for z in range(2):
            grad[z].update(far[z])
            h.append({x: grad[z][x] * gelu_slope(pre[z][x]) for x in range(-2, 6)})
        grad_edge = halo_edges(1)
        packed = edge_columns(h)
        keep_h(0, h, packed)
        fill_rows(3, 1, h)
        fill_edges(3, own_edges(packed, [grad_edge[z] * gelu_slope(pre_edge[z]) for z in range(2)]))
        grad, grad_edge = conv(3, 3, 1)

        pre, pre_edge = forward(1, 2, 1, x2)
        h = []
        for z in range(2):
            h.append({x: grad[z][x] * gelu_slope(pre[z][x]) for x in range(-1, 5)})
            h[z][-1] = h[z][-1] * up
            h[z][4] = h[z][4] * down
        packed = edge_columns(h)
        keep_h(1, h, packed)
        fill_rows(4, 0, h)
        fill_edges(4, [grad_edge[z] * gelu_slope(pre_edge[z]) * outside for z in range(2)])
        grad, _ = conv(4, 4, 0)

        pre, _ = forward(2, 3, 0, x1)
        h = [{x: grad[z][x] * gelu_slope(pre[z][x]) for x in range(4)} for z in range(2)]
        packed = edge_columns(h)
        fill_send(4, h, packed)
        start_halo(4)
        keep_h(2, h, packed)
        kernel_grad(2)
        rs_start(2)
        kernel_grad(0)
        rs_start(0)
        kernel_grad(1)
        rs_start(1)
        fill_rows(5, 0, h)
        whole_halo(4).wait_recv()
        fill_rows(5, 0, halo_rows(4))
        fill_edges(5, halo_edges(4))
        grad, _ = conv(5, 5, 0)
        for z in range(2):
            for x in range(4):
                gin_ref[pl.ds(z * 4 + x, 32, stride=8), :] = grad[z][x]
        z_start(2)
        z_start(0)
        z_start(1)
        ag_start(2)
        ag_start(0)
        ag_start(1)
        finish(2)
        finish(0)
        finish(1)
        for f in range(5):
            whole_halo(f).wait_send()
        for layer in range(3):
            rs_wait(layer).wait_send()
            z_wait(layer).wait_send()
            ag_wait(layer).wait_send()

    sequence()


def unpack_kernel(factor, gin_in, red_ref, gin_out, *refs):
    outs, held, sem = refs[0:3], refs[3:6], refs[6]
    copies = [pltpu.make_async_copy(gin_in, gin_out, sem.at[3])]
    copies[0].start()
    for layer in range(3):
        for a in range(3):
            for b in range(3):
                for c in range(3):
                    j = c * 3 + a
                    row, col = (j * 32, b * 32) if j < 8 else (b * 32, 96)
                    held[layer][9 * a + 3 * b + c] = red_ref[layer, row : row + 32, col : col + 32] * factor
        copies.append(pltpu.make_async_copy(held[layer], outs[layer], sem.at[layer]))
        copies[-1].start()
    for copy in copies:
        copy.wait()


def per_device(dims, factor, x1, x2, x3, cot, k1, k2, k3):
    flat = [v.reshape(256, 128) for v in (x3, cot, x2, x1)]
    vmem = pl.BlockSpec(memory_space=pltpu.VMEM)
    hbm = pl.BlockSpec(memory_space=pltpu.HBM)
    members = dims[3] * 2 * dims[1]
    per = 32 // members
    dma = pltpu.SemaphoreType.DMA
    gin, red = pl.pallas_call(
        functools.partial(step_kernel, dims),
        out_shape=(jax.ShapeDtypeStruct((256, 128), F32), jax.ShapeDtypeStruct((3, 32, 8, 128), F32)),
        in_specs=[hbm] * 7,
        out_specs=(vmem, vmem),
        scratch_shapes=[pltpu.VMEM((256, 128), F32)] * 4
        + [pltpu.VMEM((27, 32, 32), F32)] * 3
        + [
            pltpu.VMEM((5, 272, 128), F32),
            pltpu.VMEM((5, 480, 128), F32),
            pltpu.VMEM((6, 512, 1152), BF16),
            pltpu.VMEM((6, 192, 768), BF16),
            pltpu.VMEM((384, 640), BF16),
            pltpu.VMEM((192, 1152), F32),
            pltpu.VMEM((3, 320, 128), F32),
            pltpu.VMEM((3, 32, 8, 128), F32),
            pltpu.VMEM((3, 32, 8, 128), F32),
            pltpu.VMEM((3, dims[2], per, 8, 128), F32),
            pltpu.VMEM((3, 32, 8, 128), F32),
            dma((7,)), dma((5,)), dma((5,)), dma((3,)), dma((3,)), dma((3,)), dma((3,)), dma((3,)), dma((3,)),
        ],
        compiler_params=pltpu.CompilerParams(
            collective_id=0, has_side_effects=True, vmem_limit_bytes=40 * 1024 * 1024
        ),
        name="step",
    )(*[pltpu.with_memory_space_constraint(v, pltpu.HBM) for v in (*flat, k3, k2, k1)])
    shape = jax.ShapeDtypeStruct(k1.shape, F32)
    gin, out3, out2, out1 = pl.pallas_call(
        functools.partial(unpack_kernel, factor),
        out_shape=(jax.ShapeDtypeStruct((256, 128), F32), shape, shape, shape),
        in_specs=[vmem] * 2,
        out_specs=(hbm,) * 4,
        scratch_shapes=[pltpu.VMEM(k1.shape, F32)] * 3 + [dma((4,))],
        compiler_params=pltpu.CompilerParams(vmem_limit_bytes=8 * 1024 * 1024),
        name="unpack",
    )(gin, red.reshape(3, 256, 128))
    return gin.reshape(x1.shape), out1, out2, out3


def solution(mesh):
    gxn, gyn = mesh.shape["gx"], mesh.shape["gy"]
    zn = min(8, gxn // 2)
    dims = (gxn, gyn, zn, gxn // (2 * zn))
    factor = 1.0 / math.sqrt(2 * 4 * 128 * gxn * gyn)
    placed = P(None, None, "gx", "gy")
    return jax.shard_map(
        functools.partial(per_device, dims, factor),
        mesh=mesh,
        in_specs=(placed,) * 4 + (P(),) * 3,
        out_specs=(placed, P(), P(), P()),
        check_vma=False,
    )
```

```python
import functools
import math

import jax
import jax.numpy as jnp
from jax import lax
from jax.experimental import pallas as pl
from jax.experimental.pallas import tpu as pltpu
from jax.sharding import PartitionSpec as P

MESH = pl.DeviceIdType.MESH
F32, BF16 = jnp.float32, jnp.bfloat16
INV_ROOT_TWO = 0.7071067811865476
INV_ROOT_TWO_PI = 0.3989422804014327
SIDES = ((-1, -1), (0, -1), (1, -1), (-1, 1), (0, 1), (1, 1))


def gelu_slope(value):
    normal_cdf = 0.5 * (1.0 + lax.erf(value * INV_ROOT_TWO))
    density = jnp.exp(-0.5 * value * value) * INV_ROOT_TWO_PI
    return normal_cdf + value * density


def split(value):
    high = value.astype(BF16)
    low = (value - high.astype(F32)).astype(BF16)
    return high, low


def roll(value, shift):
    shift = shift % 128
    return value if shift == 0 else pltpu.roll(value, shift, 1)


def lanes(rows):
    return lax.broadcasted_iota(jnp.int32, (rows, 128), 1)


def tile_of(row):
    return (1, 2, 0, 3, None, -1, 4, -2, 5).index(row)


def step_kernel(
    dims, x3_in, cot_in, x2_in, x1_in, k3_in, k2_in, k1_in,
    gin_ref, red_ref,
    x3, cot, x2, x1, k3, k2, k1,
    send, recv, field, weights, hmat, prod, held,
    part, rs_recv, z_recv, ag_recv,
    load_sem, halo_send, halo_recv, rs_send_sem, rs_recv_sem, z_send_sem, z_recv_sem, ag_send_sem, ag_recv_sem,
):
    gxn, gyn, zn, ylo = dims
    members = ylo * 2 * gyn
    gx, gy = lax.axis_index("gx"), lax.axis_index("gy")
    core, my_z, my_y = lax.rem(gx, 2), lax.rem(lax.div(gx, 2), zn), lax.div(gx, 2 * zn)
    me = (my_y * 2 + core) * gyn + gy

    xs = min(4, gyn)
    yhi = gyn // xs
    my_x, my_yhi = lax.rem(gy, xs), lax.div(gy, xs)
    cores = [lax.rem(core + k, 2) for k in range(2)]
    lows = [lax.rem(my_y + k, ylo) for k in range(ylo)]
    highs = [lax.rem(my_yhi + k, yhi) for k in range(yhi)]
    columns = [lax.rem(my_x + k, xs) for k in range(xs)]
    order = []
    for kc in range(2):
        for kl in range(ylo):
            for kh in range(yhi):
                for kx in range(xs):
                    hops = min(kx, xs - kx) + (1 if kl else 2 * kh)
                    order.append((-hops, kc, kl, kh, kx))
    peers, alike = [], []
    for _, kc, kl, kh, kx in sorted(order):
        if kc or kl or kh or kx:
            spot = highs[kh] * xs + columns[kx]
            line = lows[kl] * 2 + cores[kc]
            at = lows[kl] * (2 * zn) + my_z * 2 + cores[kc]
            peers.append(((at, spot), line * gyn + spot))
            if kc == 0:
                alike.append((at, spot))
    z_order = sorted(range(1, zn), key=lambda k: -min(k, zn - k))
    z_peers = [(my_y * (2 * zn) + lax.rem(my_z + k, zn) * 2 + core, gy) for k in z_order]

    line_peers = []
    for _, kz, kc in sorted((-min(k, zn - k), k, c) for k in range(zn) for c in range(2)):
        if kz or kc:
            at_z = lax.rem(my_z + kz, zn)
            line_peers.append(((my_y * (2 * zn) + at_z * 2 + cores[kc], gy), cores[kc] * zn + at_z))
    plane = (peers, me, members, z_peers, my_z, zn)
    column = (line_peers, core * zn + my_z, 2 * zn, alike, my_y * gyn + gy, ylo * gyn)
    plans = [column if layer in (0,) else plane for layer in range(3)]

    def near(n, side):
        return (lax.rem(gx + n + gxn, gxn), lax.rem(gy + side + gyn, gyn))

    loads = []
    for i, (src, dst) in enumerate(
        ((x3_in, x3), (k3_in, k3), (cot_in, cot), (x2_in, x2), (x1_in, x1), (k2_in, k2), (k1_in, k1))
    ):
        copy = pltpu.make_async_copy(src, dst, load_sem.at[i])
        copy.start()
        loads.append(copy)

    barrier = pltpu.get_barrier_semaphore()
    around = [near(n, s) for n, s in SIDES] + [near(-1, 0), near(1, 0)]
    greeted = [device for device, _ in line_peers] + [device for device, _ in peers] + around
    for device in greeted:
        pl.semaphore_signal(barrier, inc=1, device_id=device, device_id_type=MESH)

    up = (gx > 0).astype(F32)
    down = (gx < gxn - 1).astype(F32)
    left = (gy > 0).astype(F32)
    right = (gy < gyn - 1).astype(F32)
    lane8, lane32 = lanes(8), lanes(32)
    zero32 = jnp.zeros((32, 128), F32)

    spot8, spot32 = lane8 % 8, lane32 % 8
    outside = jnp.where(spot8 < 3, left, jnp.where(spot8 >= 5, right, 1.0))
    outside = outside * jnp.where(lane8 < 24, up, jnp.where(lane8 >= 56, down, 1.0))
    outside = jnp.concatenate([outside] * 4, axis=0)

    def clear_padding():
        for bi in range(6):
            width = 128 * (9, 7, 5, 7, 5, 5)[bi]
            for base in (96, 224, 352, 480):
                field[bi, base : base + 32, 0:width] = jnp.zeros((32, width), BF16)

    def load_tiles(ref):
        return [{x: ref[pl.ds(z * 4 + x, 32, stride=8), :] for x in range(4)} for z in range(2)]

    def edge_columns(tiles):
        packed = []
        for z in range(2):
            total = zero32
            for row, tile in tiles[z].items():
                base = 8 * (row + 3)
                total = jnp.where((lane32 >= base + 2) & (lane32 < base + 8), roll(tile, base + 5), total)
            packed.append(total)
        return packed

    depth = (3, 2, 2, 1, 1)
    riders = {0: ((0, 2, 5), (3, 0, 1)), 1: ((1, 0, 2), (2, 4, 6)), 4: ((4, 0, 1),)}

    def fill_send(f, tiles):
        for z in range(2):
            for x in range(4):
                send[f, x * 64 + z * 32 : x * 64 + z * 32 + 32, :] = tiles[z][x]

    def within(start, size):
        return (spot8 >= start) & (spot8 < start + size)

    def fill_columns(f, packs):
        to_right = to_left = jnp.zeros((8, 128), F32)
        for g, *targets in riders[f]:
            d = depth[g]
            for z, t in enumerate(targets):
                squeezed = None
                for v in range(4):
                    term = roll(packs[g][z][8 * v : 8 * v + 8], 32 * v - 24)
                    squeezed = term if squeezed is None else squeezed + term
                to_right = jnp.where(within(t, d), roll(squeezed, t - 5 + d), to_right)
                to_left = jnp.where(within(t, d), roll(squeezed, t - 5), to_left)
        send[f, 256:264, :] = to_right
        send[f, 264:272, :] = to_left

    def fill_rows(bi, extent, tiles):
        for z in range(2):
            for row_in, tile in tiles[z].items():
                high, low = split(tile)
                for b in range(3):
                    row_out = row_in + 1 - b
                    if -extent <= row_out < 4 + extent:
                        row, col = z * 128 + b * 32, tile_of(row_out) * 128
                        field[bi, row : row + 32, col : col + 128] = high
                        field[bi, 256 + row : 288 + row, col : col + 128] = low

    def fill_edges(bi, edges):
        for z in range(2):
            for b in range(3):
                high, low = split(roll(edges[z], 8 - 8 * b))
                row = z * 128 + b * 32
                field[bi, row : row + 32, 512:640] = high
                field[bi, 256 + row : 288 + row, 512:640] = low

    def own_edges(packed, other):
        return [
            jnp.where(spot32 == 4, packed[z], jnp.where(spot32 == 3, roll(packed[z], -2), other[z]))
            for z in range(2)
        ]

    def start_halo(f):
        d = depth[f] * 64

        def go(src, dst, rows, device):
            pltpu.make_async_remote_copy(
                src_ref=send.at[f, pl.ds(src, rows)],
                dst_ref=recv.at[f, pl.ds(dst, rows)],
                send_sem=halo_send.at[f],
                recv_sem=halo_recv.at[f],
                device_id=device,
                device_id_type=MESH,
            ).start()

        if f in riders:
            for k in (0, 2, 3, 5, 1, 4):
                go(256 if k < 3 else 264, 2 * d + 8 * k, 8, near(-SIDES[k][0], -SIDES[k][1]))
        go(256 - d, 0, d, near(1, 0))
        go(0, d, d, near(-1, 0))

    def whole_halo(f):
        ref = recv.at[f, pl.ds(0, 128 * depth[f] + (48 if f in riders else 0))]
        return pltpu.make_async_remote_copy(
            src_ref=ref, dst_ref=ref, send_sem=halo_send.at[f], recv_sem=halo_recv.at[f],
            device_id=near(1, 0), device_id_type=MESH,
        )

    def halo_rows(f):
        d = depth[f]
        rows = [{}, {}]
        for z in range(2):
            for i in range(d):
                at = i * 64 + z * 32
                rows[z][i - d] = recv[f, at : at + 32, :] * up
                rows[z][4 + i] = recv[f, d * 64 + at : d * 64 + at + 32, :] * down
        return rows

    def halo_edges(f):
        carrier = {3: 0, 2: 1}.get(f, f)
        base, d = 128 * depth[carrier], depth[f]
        targets = [rider[1:] for rider in riders[carrier] if rider[0] == f][0]
        edges = []
        for t in targets:
            merged = []
            for j, ok in ((0, up), (1, None), (2, down)):
                at = base + 8 * j
                before, after = recv[carrier, at : at + 8, :], recv[carrier, at + 24 : at + 32, :]
                tile = jnp.where(within(5, d), roll(after, 5 - t) * right, 0.0)
                tile = jnp.where(within(3 - d, d), roll(before, 3 - d - t) * left, tile)
                merged.append(tile if ok is None else tile * ok)
            tiles = []
            for v in range(4):
                tile = jnp.where(lane8 < 24, roll(merged[0], -8 - 32 * v), roll(merged[1], 24 - 32 * v))
                tile = jnp.where(lane8 >= 56, roll(merged[2], 56 - 32 * v), tile)
                tiles.append(jnp.where(lane8 < 88, tile, 0.0))
            edges.append(jnp.concatenate(tiles, axis=0))
        return edges

    def row_block(kernel, a, c):
        return jnp.concatenate(
            [kernel[9 * a + 3 * b + c] for b in range(3)] + [jnp.zeros((32, 32), F32)], axis=1
        )

    def store_weights(wi, row, col, tile):
        high, low = split(tile)
        weights[wi, row : row + 32, col : col + 128] = high
        weights[wi, row : row + 32, 256 + col : 384 + col] = high
        weights[wi, row : row + 32, 512 + col : 640 + col] = low

    def build_weights(layer, kernel):
        for a in range(3):
            blocks = [row_block(kernel, a, c) for c in range(3)]
            flipped = jnp.concatenate(blocks + [zero32], axis=0).T
            for c in range(3):
                back = jnp.concatenate(
                    [
                        flipped[(2 - b) * 32 : (3 - b) * 32, (2 - c) * 32 : (3 - c) * 32]
                        for b in range(3)
                    ]
                    + [jnp.zeros((32, 32), F32)],
                    axis=1,
                )
                for z in range(2):
                    zp = a + z - 1
                    if 0 <= zp < 2:
                        store_weights(layer, c * 64 + z * 32, zp * 128, blocks[c])
                        store_weights(3 + layer, c * 64 + zp * 32, z * 128, back)

    def multiply(wi, bi, lo, hi):
        prod[bi, :, lo:hi] = jnp.dot(
            weights[wi, :, 0:512], field[bi, :, lo:hi], preferred_element_type=F32
        ) + jnp.dot(weights[wi, :, 512:768], field[bi, 0:256, lo:hi], preferred_element_type=F32)

    def conv(wi, bi, extent, done=0):
        width = 128 * (5 + 2 * extent)
        for lo in range(done, width, 256):
            multiply(wi, bi, lo, min(lo + 256, width))
        out, edges = [], []
        for z in range(2):
            row = z * 32
            p0, p1, p2 = (prod[bi, c * 64 + row : c * 64 + row + 32, 512:640] for c in range(3))
            edge = jnp.where(spot32 == 2, p0, roll(p2, -4))
            if extent:
                edges.append(p1 + roll(p0, 1) + roll(p2, -1))
            tiles = {}
            for x in range(-extent, 4 + extent):
                col = tile_of(x) * 128
                at_edge = roll(edge, -8 * (x + 3) - 2)
                before = roll(prod[bi, row : row + 32, col : col + 128], 1)
                after = roll(prod[bi, 128 + row : 160 + row, col : col + 128], -1)
                tiles[x] = (
                    prod[bi, 64 + row : 96 + row, col : col + 128]
                    + jnp.where(lane32 == 0, at_edge, before)
                    + jnp.where(lane32 == 127, at_edge, after)
                )
            out.append(tiles)
        return out, edges

    def store_h(c, z, col, tile):
        high, low = split(tile)
        row = c * 64 + z * 32
        hmat[row : row + 32, col : col + 128] = high
        hmat[192 + row : 224 + row, col : col + 128] = low

    def keep_h(layer, tiles, packed):
        for z in range(2):
            for x in range(4):
                at = (z * 5 + x) * 32
                held[layer, at : at + 32, :] = tiles[z][x]
            held[layer, z * 160 + 128 : z * 160 + 160, :] = packed[z]

    def kernel_grad(layer):
        bi = layer
        own = (lane32 >= 24) & (lane32 < 56)
        for z in range(2):
            for x in range(4):
                col, at = tile_of(x) * 128, (z * 5 + x) * 32
                tile = held[layer, at : at + 32, :]
                store_h(0, z, col, jnp.where(lane32 == 127, 0.0, roll(tile, -1)))
                store_h(1, z, col, tile)
                store_h(2, z, col, jnp.where(lane32 == 0, 0.0, roll(tile, 1)))
            packed = held[layer, z * 160 + 128 : z * 160 + 160, :]
            store_h(0, z, 512, jnp.where(own & (spot32 == 2), roll(packed, -3), 0.0))
            store_h(1, z, 512, zero32)
            store_h(2, z, 512, jnp.where(own & (spot32 == 5), roll(packed, 1), 0.0))
        contract = (((1,), (1,)), ((), ()))
        main = lax.dot_general(hmat[...], field[bi, 0:256, 0:640], contract, preferred_element_type=F32)
        rest = lax.dot_general(hmat[0:192, :], field[bi, 256:512, 0:640], contract, preferred_element_type=F32)
        total = main[0:192] + main[192:384] + rest
        blocks = []
        for c in range(3):
            top, low = total[c * 64 : c * 64 + 32], total[c * 64 + 32 : c * 64 + 64]
            blocks += [low[:, 0:128], top[:, 0:128] + low[:, 128:256], top[:, 128:256]]
        for j in range(8):
            block = blocks[j]
            if j < 3:
                block = jnp.where(lane32 >= 96, roll(blocks[8], 96 - 32 * j), block)
            part[layer, 4 * j : 4 * j + 4] = block.reshape(4, 8, 128)

    def group_copy(src, dst, send_sem, recv_sem, device):
        return pltpu.make_async_remote_copy(
            src_ref=src, dst_ref=dst, send_sem=send_sem, recv_sem=recv_sem, device_id=device, device_id_type=MESH
        )

    def rs_start(layer):
        firsts, mine, count, _, _, _ = plans[layer]
        per = 32 // count
        for device, m in firsts:
            group_copy(
                part.at[layer, pl.ds(m * per, per)], rs_recv.at[layer, pl.ds(mine * per, per)],
                rs_send_sem.at[layer], rs_recv_sem.at[layer], device,
            ).start()
        rs_recv[layer, pl.ds(mine * per, per)] = part[layer, pl.ds(mine * per, per)]

    def rs_wait(layer):
        span = pl.ds(0, 32 - 32 // plans[layer][2])
        return group_copy(
            part.at[layer, span], rs_recv.at[layer, span], rs_send_sem.at[layer], rs_recv_sem.at[layer], near(1, 0)
        )

    def z_start(layer):
        _, _, count, seconds, spot, _ = plans[layer]
        per = 32 // count
        rs_wait(layer).wait_recv()
        total = rs_recv[layer, 0:per]
        for m in range(1, count):
            total = total + rs_recv[layer, m * per : m * per + per]
        here = pl.ds(spot * per, per)
        z_recv[layer, here] = total
        for device in seconds:
            group_copy(
                z_recv.at[layer, here], z_recv.at[layer, here], z_send_sem.at[layer], z_recv_sem.at[layer], device
            ).start()

    def z_wait(layer):
        span = pl.ds(0, (plans[layer][5] - 1) * (32 // plans[layer][2]))
        return group_copy(
            z_recv.at[layer, span], z_recv.at[layer, span], z_send_sem.at[layer], z_recv_sem.at[layer], near(1, 0)
        )

    def ag_start(layer):
        firsts, mine, count, _, _, others = plans[layer]
        per = 32 // count
        z_wait(layer).wait_recv()
        total = z_recv[layer, 0:per]
        for k in range(1, others):
            total = total + z_recv[layer, k * per : k * per + per]
        here = pl.ds(mine * per, per)
        ag_recv[layer, here] = total
        for device, _ in firsts:
            group_copy(
                ag_recv.at[layer, here], ag_recv.at[layer, here], ag_send_sem.at[layer], ag_recv_sem.at[layer], device
            ).start()

    def ag_wait(layer):
        span = pl.ds(0, 32 - 32 // plans[layer][2])
        return group_copy(
            ag_recv.at[layer, span], ag_recv.at[layer, span], ag_send_sem.at[layer], ag_recv_sem.at[layer], near(1, 0)
        )

    def finish(layer):
        ag_wait(layer).wait_recv()
        red_ref[layer] = ag_recv[layer]

    def sequence():
        loads[0].wait()
        loads[4].wait()
        tiles3, tiles1 = load_tiles(x3), load_tiles(x1)
        fill_columns(0, {0: edge_columns(tiles3), 3: edge_columns(tiles1)})
        fill_send(0, tiles3)
        pl.semaphore_wait(barrier, len(greeted))
        start_halo(0)
        loads[2].wait()
        loads[3].wait()
        tiles, tiles2 = load_tiles(cot), load_tiles(x2)
        fill_columns(1, {1: edge_columns(tiles), 2: edge_columns(tiles2)})
        fill_send(1, tiles)
        start_halo(1)
        fill_send(2, tiles2)
        start_halo(2)
        fill_send(3, tiles1)
        start_halo(3)
        zero = [zero32, zero32]
        fill_rows(1, 1, tiles2)
        fill_rows(2, 0, tiles1)
        clear_padding()
        fill_rows(0, 2, tiles3)
        for at, kernel, layer in ((1, k3, 0), (5, k2, 1), (6, k1, 2)):
            loads[at].wait()
            build_weights(layer, kernel)
            multiply(layer, layer, 0, 256)

        def forward(layer, f, extent, ref):
            near_packed = edge_columns(load_tiles(ref)) if extent else zero
            whole_halo(f).wait_recv()
            rows, edges = halo_rows(f), halo_edges(f)
            fill_rows(layer, extent, rows)
            if extent:
                far_packed = edge_columns(rows)
                edges = own_edges([near_packed[z] + far_packed[z] for z in range(2)], edges)
            fill_edges(layer, edges)
            return conv(layer, layer, extent, 256)

        pre, pre_edge = forward(0, 0, 2, x3)
        whole_halo(1).wait_recv()
        grad, far = load_tiles(cot), halo_rows(1)
        h = []
        for z in range(2):
            grad[z].update(far[z])
            h.append({x: grad[z][x] * gelu_slope(pre[z][x]) for x in range(-2, 6)})
        grad_edge = halo_edges(1)
        packed = edge_columns(h)
        keep_h(0, h, packed)
        fill_rows(3, 1, h)
        fill_edges(3, own_edges(packed, [grad_edge[z] * gelu_slope(pre_edge[z]) for z in range(2)]))
        grad, grad_edge = conv(3, 3, 1)

        pre, pre_edge = forward(1, 2, 1, x2)
        h = []
        for z in range(2):
            h.append({x: grad[z][x] * gelu_slope(pre[z][x]) for x in range(-1, 5)})
            h[z][-1] = h[z][-1] * up
            h[z][4] = h[z][4] * down
        packed = edge_columns(h)
        keep_h(1, h, packed)
        fill_rows(4, 0, h)
        fill_edges(4, [grad_edge[z] * gelu_slope(pre_edge[z]) * outside for z in range(2)])
        grad, _ = conv(4, 4, 0)

        pre, _ = forward(2, 3, 0, x1)
        h = [{x: grad[z][x] * gelu_slope(pre[z][x]) for x in range(4)} for z in range(2)]
        packed = edge_columns(h)
        fill_columns(4, {4: packed})
        fill_send(4, h)
        start_halo(4)
        keep_h(2, h, packed)
        kernel_grad(2)
        rs_start(2)
        kernel_grad(0)
        rs_start(0)
        kernel_grad(1)
        rs_start(1)
        fill_rows(5, 0, h)
        z_start(2)
        whole_halo(4).wait_recv()
        fill_rows(5, 0, halo_rows(4))
        fill_edges(5, halo_edges(4))
        grad, _ = conv(5, 5, 0)
        for z in range(2):
            for x in range(4):
                gin_ref[pl.ds(z * 4 + x, 32, stride=8), :] = grad[z][x]
        z_start(0)
        z_start(1)
        ag_start(2)
        ag_start(0)
        ag_start(1)
        finish(2)
        finish(0)
        finish(1)
        for f in range(5):
            whole_halo(f).wait_send()
        for layer in range(3):
            rs_wait(layer).wait_send()
            z_wait(layer).wait_send()
            ag_wait(layer).wait_send()

    sequence()


def unpack_kernel(factor, gin_in, red_ref, gin_out, *refs):
    outs, held, sem = refs[0:3], refs[3:6], refs[6]
    copies = [pltpu.make_async_copy(gin_in, gin_out, sem.at[3])]
    copies[0].start()
    for layer in range(3):
        for a in range(3):
            for b in range(3):
                for c in range(3):
                    j = c * 3 + a
                    row, col = (j * 32, b * 32) if j < 8 else (b * 32, 96)
                    held[layer][9 * a + 3 * b + c] = red_ref[layer, row : row + 32, col : col + 32] * factor
        copies.append(pltpu.make_async_copy(held[layer], outs[layer], sem.at[layer]))
        copies[-1].start()
    for copy in copies:
        copy.wait()


def per_device(dims, factor, x1, x2, x3, cot, k1, k2, k3):
    flat = [v.reshape(256, 128) for v in (x3, cot, x2, x1)]
    vmem = pl.BlockSpec(memory_space=pltpu.VMEM)
    hbm = pl.BlockSpec(memory_space=pltpu.HBM)
    members = dims[3] * 2 * dims[1]
    rows = max(dims[2] * (32 // members), members // 2 * (16 // dims[2]))
    dma = pltpu.SemaphoreType.DMA
    gin, red = pl.pallas_call(
        functools.partial(step_kernel, dims),
        out_shape=(jax.ShapeDtypeStruct((256, 128), F32), jax.ShapeDtypeStruct((3, 32, 8, 128), F32)),
        in_specs=[hbm] * 7,
        out_specs=(vmem, vmem),
        scratch_shapes=[pltpu.VMEM((256, 128), F32)] * 4
        + [pltpu.VMEM((27, 32, 32), F32)] * 3
        + [
            pltpu.VMEM((5, 272, 128), F32),
            pltpu.VMEM((5, 480, 128), F32),
            pltpu.VMEM((6, 512, 1152), BF16),
            pltpu.VMEM((6, 192, 768), BF16),
            pltpu.VMEM((384, 640), BF16),
            pltpu.VMEM((6, 192, 1152), F32),
            pltpu.VMEM((3, 320, 128), F32),
            pltpu.VMEM((3, 32, 8, 128), F32),
            pltpu.VMEM((3, 32, 8, 128), F32),
            pltpu.VMEM((3, rows, 8, 128), F32),
            pltpu.VMEM((3, 32, 8, 128), F32),
            dma((7,)), dma((5,)), dma((5,)), dma((3,)), dma((3,)), dma((3,)), dma((3,)), dma((3,)), dma((3,)),
        ],
        compiler_params=pltpu.CompilerParams(
            collective_id=0, has_side_effects=True, vmem_limit_bytes=40 * 1024 * 1024
        ),
        name="step",
    )(*[pltpu.with_memory_space_constraint(v, pltpu.HBM) for v in (*flat, k3, k2, k1)])
    shape = jax.ShapeDtypeStruct(k1.shape, F32)
    gin, out3, out2, out1 = pl.pallas_call(
        functools.partial(unpack_kernel, factor),
        out_shape=(jax.ShapeDtypeStruct((256, 128), F32), shape, shape, shape),
        in_specs=[vmem] * 2,
        out_specs=(hbm,) * 4,
        scratch_shapes=[pltpu.VMEM(k1.shape, F32)] * 3 + [dma((4,))],
        compiler_params=pltpu.CompilerParams(vmem_limit_bytes=8 * 1024 * 1024),
        name="unpack",
    )(gin, red.reshape(3, 256, 128))
    return gin.reshape(x1.shape), out1, out2, out3


def solution(mesh):
    gxn, gyn = mesh.shape["gx"], mesh.shape["gy"]
    zn = min(8, gxn // 2)
    dims = (gxn, gyn, zn, gxn // (2 * zn))
    factor = 1.0 / math.sqrt(2 * 4 * 128 * gxn * gyn)
    placed = P(None, None, "gx", "gy")
    return jax.shard_map(
        functools.partial(per_device, dims, factor),
        mesh=mesh,
        in_specs=(placed,) * 4 + (P(),) * 3,
        out_specs=(placed, P(), P(), P()),
        check_vma=False,
    )
```

```python
import functools
import math

import jax
import jax.numpy as jnp
from jax import lax
from jax.experimental import pallas as pl
from jax.experimental.pallas import tpu as pltpu
from jax.sharding import PartitionSpec as P

MESH = pl.DeviceIdType.MESH
F32, BF16 = jnp.float32, jnp.bfloat16
INV_ROOT_TWO = 0.7071067811865476
INV_ROOT_TWO_PI = 0.3989422804014327
SIDES = ((-1, -1), (0, -1), (1, -1), (-1, 1), (0, 1), (1, 1))


def gelu_slope(value):
    normal_cdf = 0.5 * (1.0 + lax.erf(value * INV_ROOT_TWO))
    density = jnp.exp(-0.5 * value * value) * INV_ROOT_TWO_PI
    return normal_cdf + value * density


def split(value):
    high = value.astype(BF16)
    low = (value - high.astype(F32)).astype(BF16)
    return high, low


def roll(value, shift):
    shift = shift % 128
    return value if shift == 0 else pltpu.roll(value, shift, 1)


def lanes(rows):
    return lax.broadcasted_iota(jnp.int32, (rows, 128), 1)


def tile_of(row):
    return (1, 2, 0, 3, None, -1, 4, -2, 5).index(row)


def step_kernel(
    dims, x3_in, cot_in, x2_in, x1_in, k3_in, k2_in, k1_in,
    gin_ref, red_ref,
    x3, cot, x2, x1, k3, k2, k1,
    send, recv, field, weights, hmat, prod, held,
    part, rs_recv, z_recv, ag_recv,
    load_sem, halo_send, halo_recv, pack_recv, rs_send_sem, rs_recv_sem, z_send_sem, z_recv_sem, ag_send_sem, ag_recv_sem,
):
    gxn, gyn, zn, ylo = dims
    members = ylo * 2 * gyn
    gx, gy = lax.axis_index("gx"), lax.axis_index("gy")
    core, my_z, my_y = lax.rem(gx, 2), lax.rem(lax.div(gx, 2), zn), lax.div(gx, 2 * zn)
    me = (my_y * 2 + core) * gyn + gy

    xs = min(4, gyn)
    yhi = gyn // xs
    my_x, my_yhi = lax.rem(gy, xs), lax.div(gy, xs)
    cores = [lax.rem(core + k, 2) for k in range(2)]
    lows = [lax.rem(my_y + k, ylo) for k in range(ylo)]
    highs = [lax.rem(my_yhi + k, yhi) for k in range(yhi)]
    columns = [lax.rem(my_x + k, xs) for k in range(xs)]
    order = []
    for kc in range(2):
        for kl in range(ylo):
            for kh in range(yhi):
                for kx in range(xs):
                    hops = min(kx, xs - kx) + (1 if kl else 2 * kh)
                    order.append((-hops, kc, kl, kh, kx))
    peers, alike = [], []
    for _, kc, kl, kh, kx in sorted(order):
        if kc or kl or kh or kx:
            spot = highs[kh] * xs + columns[kx]
            line = lows[kl] * 2 + cores[kc]
            at = lows[kl] * (2 * zn) + my_z * 2 + cores[kc]
            peers.append(((at, spot), line * gyn + spot))
            if kc == 0:
                alike.append((at, spot))
    z_order = sorted(range(1, zn), key=lambda k: -min(k, zn - k))
    z_peers = [(my_y * (2 * zn) + lax.rem(my_z + k, zn) * 2 + core, gy) for k in z_order]

    line_peers = []
    for _, kz, kc in sorted((-min(k, zn - k), k, c) for k in range(zn) for c in range(2)):
        if kz or kc:
            at_z = lax.rem(my_z + kz, zn)
            line_peers.append(((my_y * (2 * zn) + at_z * 2 + cores[kc], gy), cores[kc] * zn + at_z))
    plane = (peers, me, members, z_peers, my_z, zn)
    column = (line_peers, core * zn + my_z, 2 * zn, alike, my_y * gyn + gy, ylo * gyn)
    plans = [column if layer in (0,) else plane for layer in range(3)]

    def near(n, side):
        return (lax.rem(gx + n + gxn, gxn), lax.rem(gy + side + gyn, gyn))

    loads = []
    for i, (src, dst) in enumerate(
        ((x3_in, x3), (k3_in, k3), (cot_in, cot), (x2_in, x2), (x1_in, x1), (k2_in, k2), (k1_in, k1))
    ):
        copy = pltpu.make_async_copy(src, dst, load_sem.at[i])
        copy.start()
        loads.append(copy)

    barrier = pltpu.get_barrier_semaphore()
    around = [near(n, s) for n, s in SIDES] + [near(-1, 0), near(1, 0)]
    greeted = [device for device, _ in line_peers] + [device for device, _ in peers] + around
    for device in greeted:
        pl.semaphore_signal(barrier, inc=1, device_id=device, device_id_type=MESH)

    up = (gx > 0).astype(F32)
    down = (gx < gxn - 1).astype(F32)
    left = (gy > 0).astype(F32)
    right = (gy < gyn - 1).astype(F32)
    lane8, lane32 = lanes(8), lanes(32)
    zero32 = jnp.zeros((32, 128), F32)

    spot8, spot32 = lane8 % 8, lane32 % 8
    outside = jnp.where(spot8 < 3, left, jnp.where(spot8 >= 5, right, 1.0))
    outside = outside * jnp.where(lane8 < 24, up, jnp.where(lane8 >= 56, down, 1.0))
    outside = jnp.concatenate([outside] * 4, axis=0)

    def clear_padding():
        for bi in range(6):
            width = 128 * (9, 7, 5, 7, 5, 5)[bi]
            for base in (96, 224, 352, 480):
                field[bi, base : base + 32, 0:width] = jnp.zeros((32, width), BF16)

    def load_tiles(ref):
        return [{x: ref[pl.ds(z * 4 + x, 32, stride=8), :] for x in range(4)} for z in range(2)]

    def edge_columns(tiles):
        packed = []
        for z in range(2):
            total = zero32
            for row, tile in tiles[z].items():
                base = 8 * (row + 3)
                total = jnp.where((lane32 >= base + 2) & (lane32 < base + 8), roll(tile, base + 5), total)
            packed.append(total)
        return packed

    depth = (3, 2, 2, 1, 1)
    riders = {0: ((0, 2, 5), (3, 0, 1)), 1: ((1, 0, 2), (2, 4, 6)), 4: ((4, 0, 1),)}

    def fill_send(f, tiles):
        for z in range(2):
            for x in range(4):
                send[f, x * 64 + z * 32 : x * 64 + z * 32 + 32, :] = tiles[z][x]

    def within(start, size):
        return (spot8 >= start) & (spot8 < start + size)

    def fill_columns(f, packs):
        to_right = to_left = jnp.zeros((8, 128), F32)
        for g, *targets in riders[f]:
            d = depth[g]
            for z, t in enumerate(targets):
                squeezed = None
                for v in range(4):
                    term = roll(packs[g][z][8 * v : 8 * v + 8], 32 * v - 24)
                    squeezed = term if squeezed is None else squeezed + term
                to_right = jnp.where(within(t, d), roll(squeezed, t - 5 + d), to_right)
                to_left = jnp.where(within(t, d), roll(squeezed, t - 5), to_left)
        send[f, 256:264, :] = to_right
        send[f, 264:272, :] = to_left

    def fill_rows(bi, extent, tiles):
        for z in range(2):
            for row_in, tile in tiles[z].items():
                high, low = split(tile)
                for b in range(3):
                    row_out = row_in + 1 - b
                    if -extent <= row_out < 4 + extent:
                        row, col = z * 128 + b * 32, tile_of(row_out) * 128
                        field[bi, row : row + 32, col : col + 128] = high
                        field[bi, 256 + row : 288 + row, col : col + 128] = low

    def fill_edges(bi, edges):
        for z in range(2):
            for b in range(3):
                high, low = split(roll(edges[z], 8 - 8 * b))
                row = z * 128 + b * 32
                field[bi, row : row + 32, 512:640] = high
                field[bi, 256 + row : 288 + row, 512:640] = low

    def own_edges(packed, other):
        return [
            jnp.where(spot32 == 4, packed[z], jnp.where(spot32 == 3, roll(packed[z], -2), other[z]))
            for z in range(2)
        ]

    def start_halo(f):
        d = depth[f] * 64

        def go(src, dst, rows, device, arrival):
            pltpu.make_async_remote_copy(
                src_ref=send.at[f, pl.ds(src, rows)],
                dst_ref=recv.at[f, pl.ds(dst, rows)],
                send_sem=halo_send.at[f],
                recv_sem=arrival.at[f],
                device_id=device,
                device_id_type=MESH,
            ).start()

        if f in riders:
            for k in (0, 2, 3, 5, 1, 4):
                go(256 if k < 3 else 264, 2 * d + 8 * k, 8, near(-SIDES[k][0], -SIDES[k][1]), pack_recv)
        go(256 - d, 0, d, near(1, 0), halo_recv)
        go(0, d, d, near(-1, 0), halo_recv)

    def whole_halo(f):
        ref = recv.at[f, pl.ds(0, 128 * depth[f] + (48 if f in riders else 0))]
        return pltpu.make_async_remote_copy(
            src_ref=ref, dst_ref=ref, send_sem=halo_send.at[f], recv_sem=halo_recv.at[f],
            device_id=near(1, 0), device_id_type=MESH,
        )

    def wait_rows(f):
        ref = recv.at[f, pl.ds(0, 128 * depth[f])]
        pltpu.make_async_remote_copy(
            src_ref=ref, dst_ref=ref, send_sem=halo_send.at[f], recv_sem=halo_recv.at[f],
            device_id=near(1, 0), device_id_type=MESH,
        ).wait_recv()

    def wait_columns(f):
        ref = recv.at[f, pl.ds(128 * depth[f], 48)]
        pltpu.make_async_remote_copy(
            src_ref=ref, dst_ref=ref, send_sem=halo_send.at[f], recv_sem=pack_recv.at[f],
            device_id=near(1, 0), device_id_type=MESH,
        ).wait_recv()

    def halo_rows(f):
        d = depth[f]
        rows = [{}, {}]
        for z in range(2):
            for i in range(d):
                at = i * 64 + z * 32
                rows[z][i - d] = recv[f, at : at + 32, :] * up
                rows[z][4 + i] = recv[f, d * 64 + at : d * 64 + at + 32, :] * down
        return rows

    def halo_edges(f):
        carrier = {3: 0, 2: 1}.get(f, f)
        base, d = 128 * depth[carrier], depth[f]
        targets = [rider[1:] for rider in riders[carrier] if rider[0] == f][0]
        edges = []
        for t in targets:
            merged = []
            for j, ok in ((0, up), (1, None), (2, down)):
                at = base + 8 * j
                before, after = recv[carrier, at : at + 8, :], recv[carrier, at + 24 : at + 32, :]
                tile = jnp.where(within(5, d), roll(after, 5 - t) * right, 0.0)
                tile = jnp.where(within(3 - d, d), roll(before, 3 - d - t) * left, tile)
                merged.append(tile if ok is None else tile * ok)
            tiles = []
            for v in range(4):
                tile = jnp.where(lane8 < 24, roll(merged[0], -8 - 32 * v), roll(merged[1], 24 - 32 * v))
                tile = jnp.where(lane8 >= 56, roll(merged[2], 56 - 32 * v), tile)
                tiles.append(jnp.where(lane8 < 88, tile, 0.0))
            edges.append(jnp.concatenate(tiles, axis=0))
        return edges

    def row_block(kernel, a, c):
        return jnp.concatenate(
            [kernel[9 * a + 3 * b + c] for b in range(3)] + [jnp.zeros((32, 32), F32)], axis=1
        )

    def store_weights(wi, row, col, tile):
        high, low = split(tile)
        weights[wi, row : row + 32, col : col + 128] = high
        weights[wi, row : row + 32, 256 + col : 384 + col] = high
        weights[wi, row : row + 32, 512 + col : 640 + col] = low

    def build_weights(layer, kernel):
        for a in range(3):
            blocks = [row_block(kernel, a, c) for c in range(3)]
            flipped = jnp.concatenate(blocks + [zero32], axis=0).T
            for c in range(3):
                back = jnp.concatenate(
                    [
                        flipped[(2 - b) * 32 : (3 - b) * 32, (2 - c) * 32 : (3 - c) * 32]
                        for b in range(3)
                    ]
                    + [jnp.zeros((32, 32), F32)],
                    axis=1,
                )
                for z in range(2):
                    zp = a + z - 1
                    if 0 <= zp < 2:
                        store_weights(layer, c * 64 + z * 32, zp * 128, blocks[c])
                        store_weights(3 + layer, c * 64 + zp * 32, z * 128, back)

    def multiply(wi, bi, lo, hi):
        prod[bi, :, lo:hi] = jnp.dot(
            weights[wi, :, 0:512], field[bi, :, lo:hi], preferred_element_type=F32
        ) + jnp.dot(weights[wi, :, 512:768], field[bi, 0:256, lo:hi], preferred_element_type=F32)

    def conv(wi, bi, extent, chunks=None):
        width = 128 * (5 + 2 * extent)
        for lo, hi in chunks or [(lo, min(lo + 256, width)) for lo in range(0, width, 256)]:
            multiply(wi, bi, lo, hi)
        out, edges = [], []
        for z in range(2):
            row = z * 32
            p0, p1, p2 = (prod[bi, c * 64 + row : c * 64 + row + 32, 512:640] for c in range(3))
            edge = jnp.where(spot32 == 2, p0, roll(p2, -4))
            if extent:
                edges.append(p1 + roll(p0, 1) + roll(p2, -1))
            tiles = {}
            for x in range(-extent, 4 + extent):
                col = tile_of(x) * 128
                at_edge = roll(edge, -8 * (x + 3) - 2)
                before = roll(prod[bi, row : row + 32, col : col + 128], 1)
                after = roll(prod[bi, 128 + row : 160 + row, col : col + 128], -1)
                tiles[x] = (
                    prod[bi, 64 + row : 96 + row, col : col + 128]
                    + jnp.where(lane32 == 0, at_edge, before)
                    + jnp.where(lane32 == 127, at_edge, after)
                )
            out.append(tiles)
        return out, edges

    def store_h(c, z, col, tile):
        high, low = split(tile)
        row = c * 64 + z * 32
        hmat[row : row + 32, col : col + 128] = high
        hmat[192 + row : 224 + row, col : col + 128] = low

    def keep_h(layer, tiles, packed):
        for z in range(2):
            for x in range(4):
                at = (z * 5 + x) * 32
                held[layer, at : at + 32, :] = tiles[z][x]
            held[layer, z * 160 + 128 : z * 160 + 160, :] = packed[z]

    def kernel_grad(layer):
        bi = layer
        own = (lane32 >= 24) & (lane32 < 56)
        for z in range(2):
            for x in range(4):
                col, at = tile_of(x) * 128, (z * 5 + x) * 32
                tile = held[layer, at : at + 32, :]
                store_h(0, z, col, jnp.where(lane32 == 127, 0.0, roll(tile, -1)))
                store_h(1, z, col, tile)
                store_h(2, z, col, jnp.where(lane32 == 0, 0.0, roll(tile, 1)))
            packed = held[layer, z * 160 + 128 : z * 160 + 160, :]
            store_h(0, z, 512, jnp.where(own & (spot32 == 2), roll(packed, -3), 0.0))
            store_h(1, z, 512, zero32)
            store_h(2, z, 512, jnp.where(own & (spot32 == 5), roll(packed, 1), 0.0))
        contract = (((1,), (1,)), ((), ()))
        main = lax.dot_general(hmat[...], field[bi, 0:256, 0:640], contract, preferred_element_type=F32)
        rest = lax.dot_general(hmat[0:192, :], field[bi, 256:512, 0:640], contract, preferred_element_type=F32)
        total = main[0:192] + main[192:384] + rest
        blocks = []
        for c in range(3):
            top, low = total[c * 64 : c * 64 + 32], total[c * 64 + 32 : c * 64 + 64]
            blocks += [low[:, 0:128], top[:, 0:128] + low[:, 128:256], top[:, 128:256]]
        for j in range(8):
            block = blocks[j]
            if j < 3:
                block = jnp.where(lane32 >= 96, roll(blocks[8], 96 - 32 * j), block)
            part[layer, 4 * j : 4 * j + 4] = block.reshape(4, 8, 128)

    def group_copy(src, dst, send_sem, recv_sem, device):
        return pltpu.make_async_remote_copy(
            src_ref=src, dst_ref=dst, send_sem=send_sem, recv_sem=recv_sem, device_id=device, device_id_type=MESH
        )

    def rs_start(layer):
        firsts, mine, count, _, _, _ = plans[layer]
        per = 32 // count
        for device, m in firsts:
            group_copy(
                part.at[layer, pl.ds(m * per, per)], rs_recv.at[layer, pl.ds(mine * per, per)],
                rs_send_sem.at[layer], rs_recv_sem.at[layer], device,
            ).start()
        rs_recv[layer, pl.ds(mine * per, per)] = part[layer, pl.ds(mine * per, per)]

    def rs_wait(layer):
        span = pl.ds(0, 32 - 32 // plans[layer][2])
        return group_copy(
            part.at[layer, span], rs_recv.at[layer, span], rs_send_sem.at[layer], rs_recv_sem.at[layer], near(1, 0)
        )

    def z_start(layer):
        _, _, count, seconds, spot, _ = plans[layer]
        per = 32 // count
        rs_wait(layer).wait_recv()
        total = rs_recv[layer, 0:per]
        for m in range(1, count):
            total = total + rs_recv[layer, m * per : m * per + per]
        here = pl.ds(spot * per, per)
        z_recv[layer, here] = total
        for device in seconds:
            group_copy(
                z_recv.at[layer, here], z_recv.at[layer, here], z_send_sem.at[layer], z_recv_sem.at[layer], device
            ).start()

    def z_wait(layer):
        span = pl.ds(0, (plans[layer][5] - 1) * (32 // plans[layer][2]))
        return group_copy(
            z_recv.at[layer, span], z_recv.at[layer, span], z_send_sem.at[layer], z_recv_sem.at[layer], near(1, 0)
        )

    def ag_start(layer):
        firsts, mine, count, _, _, others = plans[layer]
        per = 32 // count
        z_wait(layer).wait_recv()
        total = z_recv[layer, 0:per]
        for k in range(1, others):
            total = total + z_recv[layer, k * per : k * per + per]
        here = pl.ds(mine * per, per)
        ag_recv[layer, here] = total
        for device, _ in firsts:
            group_copy(
                ag_recv.at[layer, here], ag_recv.at[layer, here], ag_send_sem.at[layer], ag_recv_sem.at[layer], device
            ).start()

    def ag_wait(layer):
        span = pl.ds(0, 32 - 32 // plans[layer][2])
        return group_copy(
            ag_recv.at[layer, span], ag_recv.at[layer, span], ag_send_sem.at[layer], ag_recv_sem.at[layer], near(1, 0)
        )

    def finish(layer):
        ag_wait(layer).wait_recv()
        red_ref[layer] = ag_recv[layer]

    def sequence():
        loads[0].wait()
        loads[4].wait()
        tiles3, tiles1 = load_tiles(x3), load_tiles(x1)
        fill_columns(0, {0: edge_columns(tiles3), 3: edge_columns(tiles1)})
        fill_send(0, tiles3)
        pl.semaphore_wait(barrier, len(greeted))
        start_halo(0)
        loads[2].wait()
        loads[3].wait()
        tiles, tiles2 = load_tiles(cot), load_tiles(x2)
        fill_columns(1, {1: edge_columns(tiles), 2: edge_columns(tiles2)})
        fill_send(1, tiles)
        start_halo(1)
        fill_send(2, tiles2)
        start_halo(2)
        fill_send(3, tiles1)
        start_halo(3)
        zero = [zero32, zero32]
        fill_rows(1, 1, tiles2)
        fill_rows(2, 0, tiles1)
        clear_padding()
        fill_rows(0, 2, tiles3)
        for at, kernel, layer in ((1, k3, 0), (5, k2, 1), (6, k1, 2)):
            loads[at].wait()
            build_weights(layer, kernel)
            multiply(layer, layer, 0, 256)

        def forward(layer, f, extent, ref):
            near_packed = edge_columns(load_tiles(ref)) if extent else zero
            wait_rows(f)
            rows = halo_rows(f)
            fill_rows(layer, extent, rows)
            multiply(layer, layer, 256, 512)
            for lo in range(640, 640 + 256 * extent, 256):
                multiply(layer, layer, lo, lo + 256)
            if f == 0:
                wait_columns(0)
            edges = halo_edges(f)
            if extent:
                far_packed = edge_columns(rows)
                edges = own_edges([near_packed[z] + far_packed[z] for z in range(2)], edges)
            fill_edges(layer, edges)
            return conv(layer, layer, extent, ((512, 640),))

        pre, pre_edge = forward(0, 0, 2, x3)
        wait_rows(1)
        wait_columns(1)
        grad, far = load_tiles(cot), halo_rows(1)
        h = []
        for z in range(2):
            grad[z].update(far[z])
            h.append({x: grad[z][x] * gelu_slope(pre[z][x]) for x in range(-2, 6)})
        grad_edge = halo_edges(1)
        packed = edge_columns(h)
        keep_h(0, h, packed)
        fill_rows(3, 1, h)
        fill_edges(3, own_edges(packed, [grad_edge[z] * gelu_slope(pre_edge[z]) for z in range(2)]))
        grad, grad_edge = conv(3, 3, 1)

        pre, pre_edge = forward(1, 2, 1, x2)
        h = []
        for z in range(2):
            h.append({x: grad[z][x] * gelu_slope(pre[z][x]) for x in range(-1, 5)})
            h[z][-1] = h[z][-1] * up
            h[z][4] = h[z][4] * down
        packed = edge_columns(h)
        keep_h(1, h, packed)
        fill_rows(4, 0, h)
        fill_edges(4, [grad_edge[z] * gelu_slope(pre_edge[z]) * outside for z in range(2)])
        grad, _ = conv(4, 4, 0)

        pre, _ = forward(2, 3, 0, x1)
        h = [{x: grad[z][x] * gelu_slope(pre[z][x]) for x in range(4)} for z in range(2)]
        packed = edge_columns(h)
        fill_columns(4, {4: packed})
        fill_send(4, h)
        start_halo(4)
        keep_h(2, h, packed)
        kernel_grad(2)
        rs_start(2)
        kernel_grad(0)
        rs_start(0)
        kernel_grad(1)
        rs_start(1)
        fill_rows(5, 0, h)
        z_start(2)
        z_start(0)
        z_start(1)
        wait_rows(4)
        wait_columns(4)
        fill_rows(5, 0, halo_rows(4))
        fill_edges(5, halo_edges(4))
        grad, _ = conv(5, 5, 0)
        for z in range(2):
            for x in range(4):
                gin_ref[pl.ds(z * 4 + x, 32, stride=8), :] = grad[z][x]
        ag_start(2)
        ag_start(0)
        ag_start(1)
        finish(2)
        finish(0)
        finish(1)
        for f in range(5):
            whole_halo(f).wait_send()
        for layer in range(3):
            rs_wait(layer).wait_send()
            z_wait(layer).wait_send()
            ag_wait(layer).wait_send()

    sequence()


def unpack_kernel(factor, gin_in, red_ref, gin_out, *refs):
    outs, held, sem = refs[0:3], refs[3:6], refs[6]
    copies = [pltpu.make_async_copy(gin_in, gin_out, sem.at[3])]
    copies[0].start()
    for layer in range(3):
        for a in range(3):
            for b in range(3):
                for c in range(3):
                    j = c * 3 + a
                    row, col = (j * 32, b * 32) if j < 8 else (b * 32, 96)
                    held[layer][9 * a + 3 * b + c] = red_ref[layer, row : row + 32, col : col + 32] * factor
        copies.append(pltpu.make_async_copy(held[layer], outs[layer], sem.at[layer]))
        copies[-1].start()
    for copy in copies:
        copy.wait()


def per_device(dims, factor, x1, x2, x3, cot, k1, k2, k3):
    flat = [v.reshape(256, 128) for v in (x3, cot, x2, x1)]
    vmem = pl.BlockSpec(memory_space=pltpu.VMEM)
    hbm = pl.BlockSpec(memory_space=pltpu.HBM)
    members = dims[3] * 2 * dims[1]
    rows = max(dims[2] * (32 // members), members // 2 * (16 // dims[2]))
    dma = pltpu.SemaphoreType.DMA
    gin, red = pl.pallas_call(
        functools.partial(step_kernel, dims),
        out_shape=(jax.ShapeDtypeStruct((256, 128), F32), jax.ShapeDtypeStruct((3, 32, 8, 128), F32)),
        in_specs=[hbm] * 7,
        out_specs=(vmem, vmem),
        scratch_shapes=[pltpu.VMEM((256, 128), F32)] * 4
        + [pltpu.VMEM((27, 32, 32), F32)] * 3
        + [
            pltpu.VMEM((5, 272, 128), F32),
            pltpu.VMEM((5, 480, 128), F32),
            pltpu.VMEM((6, 512, 1152), BF16),
            pltpu.VMEM((6, 192, 768), BF16),
            pltpu.VMEM((384, 640), BF16),
            pltpu.VMEM((6, 192, 1152), F32),
            pltpu.VMEM((3, 320, 128), F32),
            pltpu.VMEM((3, 32, 8, 128), F32),
            pltpu.VMEM((3, 32, 8, 128), F32),
            pltpu.VMEM((3, rows, 8, 128), F32),
            pltpu.VMEM((3, 32, 8, 128), F32),
            dma((7,)), dma((5,)), dma((5,)), dma((5,)), dma((3,)), dma((3,)), dma((3,)), dma((3,)), dma((3,)), dma((3,)),
        ],
        compiler_params=pltpu.CompilerParams(
            collective_id=0, has_side_effects=True, vmem_limit_bytes=40 * 1024 * 1024
        ),
        name="step",
    )(*[pltpu.with_memory_space_constraint(v, pltpu.HBM) for v in (*flat, k3, k2, k1)])
    shape = jax.ShapeDtypeStruct(k1.shape, F32)
    gin, out3, out2, out1 = pl.pallas_call(
        functools.partial(unpack_kernel, factor),
        out_shape=(jax.ShapeDtypeStruct((256, 128), F32), shape, shape, shape),
        in_specs=[vmem] * 2,
        out_specs=(hbm,) * 4,
        scratch_shapes=[pltpu.VMEM(k1.shape, F32)] * 3 + [dma((4,))],
        compiler_params=pltpu.CompilerParams(vmem_limit_bytes=8 * 1024 * 1024),
        name="unpack",
    )(gin, red.reshape(3, 256, 128))
    return gin.reshape(x1.shape), out1, out2, out3


def solution(mesh):
    gxn, gyn = mesh.shape["gx"], mesh.shape["gy"]
    zn = min(8, gxn // 2)
    dims = (gxn, gyn, zn, gxn // (2 * zn))
    factor = 1.0 / math.sqrt(2 * 4 * 128 * gxn * gyn)
    placed = P(None, None, "gx", "gy")
    return jax.shard_map(
        functools.partial(per_device, dims, factor),
        mesh=mesh,
        in_specs=(placed,) * 4 + (P(),) * 3,
        out_specs=(placed, P(), P(), P()),
        check_vma=False,
    )
```
